256 devices in a mesh: seq: 32 (over y, z), mp: 8 (over x, core).
Axes of the slice: x: 4, y: 4, z: 8, core: 2. Of those that a mesh axis runs over, the one named last changes fastest.
Arguments:
- out_grad: bfloat16 [16384, 8192], P('seq', 'mp'), may hold values from -6 to 6
- out_weight: bfloat16 [4096, 8192], P('mp'), may hold values from -0.0625 to 0.0625
- queries: bfloat16 [16384, 4096], P('seq', 'mp'), may hold values from -5 to 5
- keys: bfloat16 [64, 128, 4096], P('seq', None, 'mp'), may hold values from -5 to 5
- values: bfloat16 [64, 128, 4096], P('seq', None, 'mp'), may hold values from -6 to 6
- retrieval: int32 [256, 2], replicated, may hold values from 0 to 63, as said below
- counts: int32 [256], P('seq'), may hold values from 1 to 2
Outputs:
- query_grad: bfloat16 [16384, 4096], P('seq', 'mp')
- key_grad: bfloat16 [64, 128, 4096], P('seq', None, 'mp')
- value_grad: bfloat16 [64, 128, 4096], P('seq', None, 'mp')
The draws below stay inside these ranges and needn't reach their ends.
Inputs may be any that keep to these rules, and one draw needn't show every extreme that they name: `retrieval`: entry e is held by index e // 2 of seq. The 16 neighbour places of one index's blocks name entries of any one owner at most 1 times, and some owner is named exactly 1 times by the blocks of every index.
All inputs are finite; a program needn't handle non-finite values.
Results may differ from the reference program's by a relative error of at most 0.0091.
Values may be sent and summed in bfloat16 or wider, within the bound.
A program may use at most 128 MiB of HBM per device.

```python
import math
import jax
import jax.numpy as jnp
from jax import lax

D = 8192
HEADS = 32
HEAD = 128
BLOCK = 64
NEIGH = 2
NROW = 128
TOK_DEV = 512
NEI_DEV = 2
TOKENS = 16384
CH_DEV = 8
BLOCKS = 256
SLOTS_DEV = 16
CAP = 1
ENTRIES = 64
N_SEQ = 32


def draw_queries(key, part):
    shape = (TOK_DEV * N_SEQ, HEADS * HEAD)
    own_key = jax.random.fold_in(key, 1)
    result = jax.random.truncated_normal(own_key, -5.0, 5.0, shape, jnp.float32)
    return result.astype(jnp.bfloat16)


def draw_keys(key, part):
    shape = (NEI_DEV * N_SEQ, NROW, HEADS * HEAD)
    own_key = jax.random.fold_in(key, 2)
    result = jax.random.truncated_normal(own_key, -5.0, 5.0, shape, jnp.float32)
    return result.astype(jnp.bfloat16)


def draw_retrieval(key, part):
    readers = BLOCKS // CH_DEV
    slot_total = SLOTS_DEV
    slot_cap = CAP
    hot_owner = jax.random.randint(jax.random.fold_in(key, 11), (), 0, readers)

    def other_order(sub_key):
        return jax.random.permutation(sub_key, readers - 1)

    def slot_order(sub_key):
        return jax.random.permutation(sub_key, slot_total)
    others = jax.vmap(other_order)(jax.random.split(jax.random.fold_in(key, 12), readers))
    place = jnp.arange(slot_total)
    spread = max(slot_total - slot_cap, 1)
    group = jnp.where(place < slot_cap, 0, 1 + (place - slot_cap) * (readers - 1) // spread)
    group_index = jnp.broadcast_to(jnp.maximum(group - 1, 0)[None, :], (readers, slot_total))
    picked = jnp.take_along_axis(others, group_index, axis=1)
    owners = jnp.where(group[None, :] == 0, hot_owner, (hot_owner + 1 + picked) % readers)
    shuffles = jax.vmap(slot_order)(jax.random.split(jax.random.fold_in(key, 13), readers))
    owners = jnp.take_along_axis(owners, shuffles, axis=1)
    local_ids = jax.random.randint(jax.random.fold_in(key, 14), (readers, slot_total), 0, NEI_DEV)
    return (owners * NEI_DEV + local_ids).reshape(BLOCKS, NEIGH).astype(jnp.int32)


def with_ends(values, key, least, largest):
    longest = values.shape.index(max(values.shape))
    spots = []
    for shift in (0, 1):
        where = [jax.random.randint(jax.random.fold_in(key, axis), (), 0, length) for axis, length in enumerate(values.shape)]
        where[longest] = (where[longest] + shift) % values.shape[longest]
        spots.append(tuple(where))
    return values.at[spots[0]].set(least).at[spots[1]].set(largest)


def block_scale(rng, shape, cuts, low, largest):
    def one(axis_at, parts):
        steps = jax.random.uniform(jax.random.fold_in(jax.random.fold_in(rng, 6), axis_at), (parts,), jnp.float32, low / len(cuts), largest / len(cuts))
        return jnp.repeat(jnp.exp(steps), shape[axis_at] // parts).reshape((-1,) + (1,) * (len(shape) - axis_at - 1))

    gain = one(*cuts[0])
    for cut in cuts[1:]:
        gain = gain * one(*cut)
    return gain


def noise(stream_key, shape, deviation, bound, cuts=(), held_as=jnp.bfloat16):
    factor_of = block_scale(stream_key, shape, cuts, -0.22, 0.18) if cuts else 1.0
    array = jax.random.normal(stream_key, shape, jnp.float32) * deviation * factor_of
    return jnp.minimum(jnp.maximum(array, -bound), bound).astype(held_as)


def setup_inputs(seed: int = 0) -> dict:
    key_of = jax.random.split(jax.random.key(seed), 8)
    return {
        "out_grad": noise(key_of[0], (TOKENS, D), 1.0, 6.0, ((0, 32), (1, 8))),
        "out_weight": noise(key_of[1], (HEADS * HEAD, D), D ** -0.5, 0.0625, ((0, 8),)),
        "queries": draw_queries(jax.random.fold_in(key_of[7], 71), 0),
        "keys": draw_keys(jax.random.fold_in(key_of[7], 71), 0),
        "values": noise(key_of[4], (ENTRIES, NROW, HEADS * HEAD), 1.0, 6.0, ((0, 32), (2, 8))),
        "retrieval": draw_retrieval(jax.random.fold_in(key_of[7], 71), 0),
        "counts": with_ends(jax.random.randint(key_of[6], (BLOCKS,), 1, NEIGH + 1), jax.random.fold_in(key_of[6], 1), 1, NEIGH).astype(jnp.int32),
    }


def block_terms(query_rows, grad_rows, key_rows, value_rows, live_keys):
    score_scale = 1.0 / math.sqrt(HEAD)
    scores = jnp.einsum('qhe,khe->hqk', query_rows.astype(jnp.float32), key_rows.astype(jnp.float32)) * score_scale
    live_mask = live_keys[None, None, :]
    row_max = lax.optimization_barrier(jnp.max(jnp.where(live_mask, scores, -jnp.inf), axis=-1, keepdims=True))
    raised = jnp.where(live_mask, jnp.exp(scores - row_max), 0.0)
    attn_weights = raised / lax.optimization_barrier(jnp.sum(raised, axis=-1, keepdims=True))
    weights_low = attn_weights.astype(jnp.bfloat16)
    attn_out = jnp.einsum('hqk,khe->qhe', weights_low.astype(jnp.float32), value_rows.astype(jnp.float32))
    row_dot = lax.optimization_barrier(jnp.sum(grad_rows.astype(jnp.float32) * attn_out, axis=-1))
    grad_weights = jnp.einsum('qhe,khe->hqk', grad_rows.astype(jnp.float32), value_rows.astype(jnp.float32))
    grad_scores = attn_weights * (grad_weights - jnp.transpose(row_dot, (1, 0))[:, :, None])
    grad_low = grad_scores.astype(jnp.bfloat16).astype(jnp.float32)
    query_grad = (jnp.einsum('hqk,khe->qhe', grad_low, key_rows.astype(jnp.float32)) * score_scale).astype(jnp.bfloat16)
    key_terms = (jnp.einsum('hqk,qhe->khe', grad_low, query_rows.astype(jnp.float32)) * score_scale).astype(jnp.bfloat16)
    value_terms = jnp.einsum('hqk,qhe->khe', weights_low.astype(jnp.float32), grad_rows.astype(jnp.float32)).astype(jnp.bfloat16)
    return (query_grad, key_terms, value_terms)

def reference(out_grad, out_weight, queries, keys, values, retrieval, counts):
    head_cols = HEADS * HEAD
    grad_out = jnp.dot(out_grad, out_weight.T, preferred_element_type=jnp.float32).astype(jnp.bfloat16)
    query_view = queries.reshape(BLOCKS, BLOCK, HEADS, HEAD)
    grad_view = grad_out.reshape(BLOCKS, BLOCK, HEADS, HEAD)

    def step_fn(carry, inputs):
        key_acc, value_acc = carry
        query_rows, grad_rows, lists, count_now = inputs
        key_rows = jnp.take(keys, lists, axis=0).reshape(NEIGH * NROW, HEADS, HEAD)
        value_rows = jnp.take(values, lists, axis=0).reshape(NEIGH * NROW, HEADS, HEAD)
        live_keys = jnp.arange(NEIGH * NROW, dtype=jnp.int32) < count_now * NROW
        query_grad, key_terms, value_terms = block_terms(query_rows, grad_rows, key_rows, value_rows, live_keys)
        key_acc = key_acc.at[lists].add(key_terms.reshape(NEIGH, NROW, head_cols).astype(jnp.float32))
        value_acc = value_acc.at[lists].add(value_terms.reshape(NEIGH, NROW, head_cols).astype(jnp.float32))
        return ((key_acc, value_acc), query_grad)
    start_acc = (jnp.zeros((ENTRIES, NROW, head_cols), jnp.float32), jnp.zeros((ENTRIES, NROW, head_cols), jnp.float32))
    final_acc, query_grads = lax.scan(step_fn, start_acc, (query_view, grad_view, retrieval, counts))
    key_acc, value_acc = final_acc
    return (query_grads.reshape(TOKENS, head_cols), key_acc.astype(jnp.bfloat16), value_acc.astype(jnp.bfloat16))
```

```python
import functools
import math

import jax
import jax.numpy as jnp
from jax import lax
from jax.experimental import pallas as pl
from jax.experimental.pallas import tpu as pltpu
from jax.sharding import PartitionSpec as P

HEAD = 128
BLOCK = 64
NEIGH = 2
NX, NY, NZ = 4, 4, 8
OWN = NZ
RDR = NY
LOW = -1e30
MESH = pl.DeviceIdType.MESH
F32, BF16 = jnp.float32, jnp.bfloat16
NT = (((1,), (1,)), ((), ()))
NN = (((1,), (0,)), ((), ()))
TN = (((0,), (0,)), ((), ()))


class Ids:
    def __init__(self):
        self.at = {}

    def __call__(self, *name):
        return self.at.setdefault(name, len(self.at))


MAX_COPIES = 112


def body(
    heads,
    scal,
    vec,
    cnt_in,
    og_in,
    w_in,
    q_in,
    k_in,
    v_in,
    dq_out,
    dk_out,
    dv_out,
    og,
    w,
    acc,
    kv,
    q_all,
    do_all,
    cnt_all,
    q_own,
    do_own,
    ex,
    gw,
    st1,
    st2,
    fac,
    dqp,
    dkv,
    rsr,
    rsl,
    dqb,
    dq_r,
    dq_l,
    ssem,
    rsem,
    lsem,
):
    ids = Ids()
    scale = 1.0 / math.sqrt(HEAD)
    seq, mp = lax.axis_index("seq"), lax.axis_index("mp")
    y, z = seq // NZ, seq % NZ
    x, core = mp // 2, mp % 2
    half = BLOCK * 4

    def at_x(d):
        return (seq, ((x + d) % NX) * 2 + core)

    sibling = (seq, x * 2 + (1 - core))

    def at_y(d):
        return (((y + d) % NY) * NZ + z, mp)

    def at_z(d):
        return (y * NZ + (z + d) % NZ, mp)

    def zz(d):
        return (z + d) % NZ

    started = []

    def send(name, src, dst, dev):
        i = ids(*name)
        cp = pltpu.make_async_remote_copy(
            src_ref=src, dst_ref=dst, send_sem=ssem.at[i], recv_sem=rsem.at[i], device_id=dev, device_id_type=MESH
        )
        cp.start()
        started.append(cp)

    def recv(name, dst):
        i = ids(*name)
        pltpu.make_async_remote_copy(
            src_ref=dst, dst_ref=dst, send_sem=ssem.at[i], recv_sem=rsem.at[i], device_id=sibling, device_id_type=MESH
        ).wait_recv()

    barrier = pltpu.get_barrier_semaphore()
    peers = [at_x(1), at_x(-1), sibling, at_y(1), at_y(-1), at_y(2), at_z(1), at_z(-1)]
    for dev in peers:
        pl.semaphore_signal(barrier, inc=1, device_id=dev, device_id_type=MESH)

    local = []

    def local_copy(src, dst):
        cp = pltpu.make_async_copy(src, dst, lsem.at[len(local)])
        cp.start()
        local.append(cp)

    local_copy(og_in, og.at[mp])
    for c in range(2 * NX):
        local_copy(w_in.at[:, pl.ds(c * 1024, 1024)], w.at[c])
    local_copy(q_in, q_all.at[pl.ds(y * 8, 8)])
    local_copy(k_in, kv.at[0, z])
    local_copy(v_in, kv.at[1, z])
    local_copy(cnt_in, cnt_all.at[pl.ds(y * 8, 8)])

    pl.semaphore_wait(barrier, len(peers))

    def kv_piece(a, o, e):
        return kv.at[a, o, pl.ds(e * 128, 128)]

    pieces = [(a, e) for a in range(2) for e in range(2)]

    def kv_first():
        for a, e in pieces:
            src = (k_in, v_in)[a].at[pl.ds(e * 128, 128)]
            send(("kvR", 1, a, e), src, kv_piece(a, z, e), at_z(1))
            send(("kvL", 1, a, e), src, kv_piece(a, z, e), at_z(-1))

    def kv_hop(k):
        for a, e in pieces:
            if k < 4 or e == 0:
                o = zz(-k)
                recv(("kvR", k, a, e), kv_piece(a, o, e))
                if k < 3 or (k == 3 and e == 0):
                    send(("kvR", k + 1, a, e), kv_piece(a, o, e), kv_piece(a, o, e), at_z(1))
            if k < 4 or e == 1:
                o = zz(k)
                recv(("kvL", k, a, e), kv_piece(a, o, e))
                if k < 3 or (k == 3 and e == 1):
                    send(("kvL", k + 1, a, e), kv_piece(a, o, e), kv_piece(a, o, e), at_z(-1))

    def y_rows(d, h):
        return pl.ds(((y + d) % NY) * 8 + h * 4, 4)

    def y_first(tag, src, buf, h):
        send((tag, "R", h), src, buf.at[y_rows(0, h)], at_y(1))
        send((tag, "L", h), src, buf.at[y_rows(0, h)], at_y(-1))

    def y_on(tag, buf, h):
        d = -1 if h == 0 else 1
        rows = buf.at[y_rows(d, h)]
        recv((tag, "R" if h == 0 else "L", h), rows)
        send((tag, "F", h), rows, rows, at_y(1 if h == 0 else -1))

    def y_rest(tag, buf, h):
        d = 1 if h == 0 else -1
        recv((tag, "L" if h == 0 else "R", h), buf.at[y_rows(d, h)])
        recv((tag, "F", h), buf.at[y_rows(2, h)])

    def y_direct(tag, src, buf, rows):
        mine = buf.at[pl.ds(y * rows, rows)]
        for d in (1, -1, 2):
            send((tag, d), src if src is not None else mine, mine, at_y(d))

    def y_direct_wait(tag, buf, rows):
        for d in (1, -1, 2):
            recv((tag, d), buf.at[pl.ds(((y - d) % NY) * rows, rows)])

    def og_piece(d, h, other=False):
        c = ((x + d) % NX) * 2 + ((1 - core) if other else core)
        return og.at[c, pl.ds(h * half, half)]

    def x_own(h, way):
        src = og_in.at[pl.ds(h * half, half)]
        send(("og", way, h), src, og_piece(0, h), at_x(1 if way == "R" else -1))

    def x_pass(d, h):
        if d == -1:
            name = ("og", "R", h)
        elif d == 1:
            name = ("og", "L", h)
        else:
            name = ("og", "F", h)
        piece = og_piece(d, h)
        recv(name, piece)
        if (d, h) == (-1, 0):
            send(("og", "F", h), piece, piece, at_x(1))
        if (d, h) == (1, 1):
            send(("og", "F", h), piece, piece, at_x(-1))
        send(("ogc", d, h), piece, piece, sibling)

    def x_sib(d, h):
        recv(("ogc", d, h), og_piece(d, h, True))

    def mm(d, h, other, first=False):
        c = ((x + d) % NX) * 2 + ((1 - core) if other else core)
        t = lax.dot_general(og[c, pl.ds(h * half, half), :], w[c], NT, preferred_element_type=F32)
        if first:
            acc[h] = t
        else:
            acc[h] += t

    def grad_done(h):
        do_all[pl.ds(y * 8 + h * 4, 4)] = acc[h].astype(BF16).reshape(4, BLOCK, heads * HEAD)
        y_first("do", do_all.at[y_rows(0, h)], do_all, h)

    lane_reader = lax.broadcasted_iota(jnp.int32, (8, RDR * BLOCK), 1) // BLOCK

    def gather_blocks(src, dst):
        def one(o, carry):
            for r in range(RDR):
                dst[o, pl.ds(r * BLOCK, BLOCK), :] = src[scal[o * RDR + r]]
            return carry

        lax.fori_loop(0, OWN, one, 0)

    def partner_rows(buf, o, base):
        t = buf[scal[base + o * RDR]]
        for r in range(1, RDR):
            t = jnp.where(lane_reader == r, buf[scal[base + o * RDR + r]], t)
        return t

    def cols(h):
        return pl.ds(h * HEAD, HEAD)

    def score_one(o):
        par = vec[o, 2:3, :]
        for h in range(heads):
            s = lax.dot_general(kv[0, o, :, cols(h)], q_own[o, :, cols(h)], NT, preferred_element_type=F32)
            s = jnp.where(par > 0.5, s[128:], s[:128]) * scale
            m = jnp.max(s, axis=0, keepdims=True)
            e = jnp.exp(s - m)
            ex[o, h] = e
            st1[y * OWN + o, h : h + 1, :] = m
            st1[y * OWN + o, heads + h : heads + h + 1, :] = jnp.sum(e, axis=0, keepdims=True)

    def scores(dist):
        if dist in (0, 4):
            score_one(zz(dist))
        else:

            def one(i, carry):
                score_one(zz(dist * (1 - 2 * i)))
                return carry

            lax.fori_loop(0, 2, one, 0)

    def lives(o):
        exists, place = vec[o, 0:1, :], vec[o, 1:2, :]
        short = 2.0 - partner_rows(cnt_all, o, 0)[0:1, :]
        return exists * (1.0 - place * short) > 0.5, exists * (1.0 - (1.0 - place) * short) > 0.5

    def factors():
        def one(o, carry):
            live, live_p = lives(o)
            own = st1[y * OWN + o]
            oth = partner_rows(st1, o, 32)
            m_o, l_o = own[:heads], own[heads : 2 * heads]
            m_p = jnp.where(live_p, oth[:heads], LOW)
            l_p = jnp.where(live_p, oth[heads : 2 * heads], 0.0)
            m = jnp.maximum(m_o, m_p)
            a = jnp.exp(m_o - m)
            f = jnp.where(live, a / (l_o * a + l_p * jnp.exp(m_p - m)), 0.0)
            par = vec[o, 2:3, :]
            fac[o, 0:heads, :] = f * (1.0 - par)
            fac[o, heads : 2 * heads, :] = f * par
            return carry

        lax.fori_loop(0, OWN, one, 0)

    def both(o, h, t0, t1):
        return jnp.concatenate([t0.astype(BF16), t1.astype(BF16)], axis=0)

    def value_one(o):
        for h in range(heads):
            e = ex[o, h]
            p = both(o, h, e * fac[o, h : h + 1, :], e * fac[o, heads + h : heads + h + 1, :])
            t = lax.dot_general(p, do_own[o, :, cols(h)], NN, preferred_element_type=F32)
            dkv[1, o, :, cols(h)] = t.astype(BF16)

    def dots_one(o):
        par = vec[o, 2:3, :]
        for h in range(heads):
            g = lax.dot_general(kv[1, o, :, cols(h)], do_own[o, :, cols(h)], NT, preferred_element_type=F32)
            g = jnp.where(par > 0.5, g[128:], g[:128])
            gw[o, h] = g
            f = fac[o, h : h + 1, :] + fac[o, heads + h : heads + h + 1, :]
            p = (ex[o, h] * f).astype(BF16).astype(F32)
            st2[y * OWN + o, h : h + 1, :] = jnp.sum(p * g, axis=0, keepdims=True)

    def key_one(o):
        _, live_p = lives(o)
        rd = st2[y * OWN + o][:heads] + jnp.where(live_p, partner_rows(st2, o, 32)[:heads], 0.0)
        for h in range(heads):
            e = ex[o, h]
            t = gw[o, h] - rd[h : h + 1]
            d = both(o, h, e * fac[o, h : h + 1, :] * t, e * fac[o, heads + h : heads + h + 1, :] * t)
            dk = lax.dot_general(d, q_own[o, :, cols(h)], NN, preferred_element_type=F32)
            dkv[0, o, :, cols(h)] = (dk * scale).astype(BF16)
            dq = lax.dot_general(d, kv[0, o, :, cols(h)], TN, preferred_element_type=F32)
            dqp[pl.ds(o * RDR, RDR), :, cols(h)] = (dq * scale).astype(BF16).reshape(RDR, BLOCK, HEAD)

    def per_owner(fn, dist):
        if dist in (0, 4):
            fn(zz(dist))
        else:

            def one(i, carry):
                fn(zz(dist * (1 - 2 * i)))
                return carry

            lax.fori_loop(0, 2, one, 0)

    def rs_buf(way, a, k, e):
        return (rsr if way == "R" else rsl).at[a, k, pl.ds(e * 128, 128)]

    def rs_hop(way, a, k, e):
        far = 0 if way == "R" else 1
        sign = 1 if way == "R" else -1
        o = zz(sign * (4 - k))
        piece = dkv.at[a, o, pl.ds(e * 128, 128)]
        if k > 1 or (k == 1 and e == far):
            rs_take(way, a, k - 1, e, o)
        send(("rs" + way, a, k, e), piece, rs_buf(way, a, k, e), at_z(sign))

    def rs_take(way, a, k, e, o):
        buf = rsr if way == "R" else rsl
        recv(("rs" + way, a, k, e), rs_buf(way, a, k, e))
        rows = pl.ds(e * 128, 128)
        dkv[a, o, rows, :] = (dkv[a, o, rows, :].astype(F32) + buf[a, k, rows, :].astype(F32)).astype(BF16)

    def rs_round(a, k):
        for e in range(2):
            for way, far in (("R", 0), ("L", 1)):
                if k > 0 or e == far:
                    rs_hop(way, a, k, e)

    kv_first()
    y_direct("cnt", cnt_in, cnt_all, 8)
    for h in range(2):
        y_first("q", q_in.at[pl.ds(h * 4, 4)], q_all, h)
    x_own(0, "R")
    x_own(0, "L")
    x_own(1, "L")
    for h in range(2):
        send(("ogc", 0, h), og_in.at[pl.ds(h * half, half)], og_piece(0, h), sibling)

    for h in range(2):
        y_on("q", q_all, h)
    for cp in local:
        cp.wait()
    for h in range(2):
        mm(0, h, False, True)
        x_sib(0, h)
        mm(0, h, True)

    kv_hop(1)
    x_pass(-1, 0)
    x_own(1, "R")
    x_pass(1, 0)
    for h in range(2):
        y_rest("q", q_all, h)
    y_direct_wait("cnt", cnt_all, 8)
    gather_blocks(q_all, q_own)
    for d in (-1, 1):
        mm(d, 0, False)
        x_sib(d, 0)
        mm(d, 0, True)
    scores(0)
    scores(1)

    kv_hop(2)
    x_pass(2, 0)
    mm(2, 0, False)
    x_sib(2, 0)
    mm(2, 0, True)
    grad_done(0)
    x_pass(1, 1)
    mm(1, 1, False)
    x_sib(1, 1)
    mm(1, 1, True)
    scores(2)
    y_on("do", do_all, 0)

    kv_hop(3)
    for d in (-1, 2):
        x_pass(d, 1)
        mm(d, 1, False)
        x_sib(d, 1)
        mm(d, 1, True)
    grad_done(1)
    scores(3)
    kv_hop(4)
    scores(4)
    y_direct("st1", None, st1, OWN)
    y_on("do", do_all, 1)
    y_rest("do", do_all, 0)
    y_direct_wait("st1", st1, OWN)
    factors()
    y_rest("do", do_all, 1)
    gather_blocks(do_all, do_own)

    per_owner(value_one, 4)
    rs_round(1, 0)
    per_owner(value_one, 3)
    rs_hop("R", 1, 1, 1)
    rs_hop("L", 1, 1, 0)
    for d in (2, 1, 0):
        per_owner(value_one, d)
    for d in (4, 3, 2):
        per_owner(dots_one, d)
    rs_hop("R", 1, 1, 0)
    rs_hop("L", 1, 1, 1)
    for d in (1, 0):
        per_owner(dots_one, d)
    y_direct("st2", None, st2, OWN)
    rs_round(1, 2)
    y_direct_wait("st2", st2, OWN)

    per_owner(key_one, 4)
    rs_round(0, 0)
    per_owner(key_one, 3)
    rs_hop("R", 0, 1, 1)
    rs_hop("L", 0, 1, 0)
    per_owner(key_one, 2)
    rs_round(1, 3)
    rs_hop("R", 0, 1, 0)
    rs_hop("L", 0, 1, 1)
    for d in (1, 0):
        per_owner(key_one, d)

    def blocks(r, carry):
        def one(b, carry2):
            j = r * 16 + b * 2
            t = dqp[scal[64 + j]].astype(F32) * scal[128 + j].astype(F32)
            t += dqp[scal[65 + j]].astype(F32) * scal[129 + j].astype(F32)
            dqb[r * 8 + b] = t.astype(BF16)
            return carry2

        return lax.fori_loop(0, 8, one, carry)

    lax.fori_loop(0, RDR, blocks, 0)

    def dq_rows(d, h):
        return dqb.at[y_rows(d, h)]

    send(("dq", "R", "far"), dq_rows(2, 0), dq_r.at[pl.ds(8, 4)], at_y(1))
    send(("dq", "L", "far"), dq_rows(2, 1), dq_l.at[pl.ds(8, 4)], at_y(-1))
    send(("dq", "R", 1), dq_rows(1, 1), dq_r.at[pl.ds(4, 4)], at_y(1))
    send(("dq", "L", 0), dq_rows(-1, 0), dq_l.at[pl.ds(0, 4)], at_y(-1))

    rs_round(0, 2)

    def dq_on(way, h, d, buf):
        recv(("dq", way, "far"), buf.at[pl.ds(8, 4)])
        rows = y_rows(d, h)
        dqb[rows] = (dqb[rows].astype(F32) + buf[pl.ds(8, 4)].astype(F32)).astype(BF16)
        send(("dq", way, h), dqb.at[rows], buf.at[pl.ds(h * 4, 4)], at_y(d))

    dq_on("R", 0, 1, dq_r)
    dq_on("L", 1, -1, dq_l)

    def rs_last(a, out):
        for e in range(2):
            rows = pl.ds(e * 128, 128)
            recv(("rsR", a, 3, e), rs_buf("R", a, 3, e))
            recv(("rsL", a, 3, e), rs_buf("L", a, 3, e))
            t = dkv[a, z, rows, :].astype(F32) + rsr[a, 3, rows, :].astype(F32) + rsl[a, 3, rows, :].astype(F32)
            out[rows, :] = t.astype(BF16)

    rs_last(1, dv_out)
    rs_round(0, 3)
    for h in range(2):
        recv(("dq", "R", h), dq_r.at[pl.ds(h * 4, 4)])
        recv(("dq", "L", h), dq_l.at[pl.ds(h * 4, 4)])
    own = dqb[pl.ds(y * 8, 8)].astype(F32)
    dq_out[...] = (own + dq_r[0:8].astype(F32) + dq_l[0:8].astype(F32)).astype(BF16)
    rs_last(0, dk_out)
    for cp in started:
        cp.wait_send()


def on_device(out_grad, out_weight, queries, keys, values, retrieval, counts):
    seq = lax.axis_index("seq")
    y, z = seq // NZ, seq % NZ
    tok, width = queries.shape
    heads = width // HEAD
    blocks = tok // BLOCK
    slots = blocks * NEIGH
    per_owner = keys.shape[0]
    lists = lax.dynamic_index_in_dim(retrieval.reshape(NY, NZ, slots), z, 1, keepdims=False)
    owner = lists // per_owner
    other = owner.reshape(NY, blocks, NEIGH)[:, :, ::-1].reshape(NY, slots)
    match = (owner[None, :, :] == (y * NZ + jnp.arange(NZ))[:, None, None]).astype(jnp.int32)
    place = jnp.arange(slots)[None, None, :]

    def pick(t):
        return jnp.sum(match * t, axis=2)

    reader = jnp.arange(NY)
    block_at = reader[None, :] * blocks + pick(place // NEIGH)
    mine = (owner // NZ == y).astype(jnp.int32)
    pair_at = jnp.where(mine > 0, owner - y * NZ, 0) * NY + reader[:, None]
    scal = jnp.concatenate(
        [block_at.reshape(-1), pick(other[None]).reshape(-1), pair_at.reshape(-1), mine.reshape(-1)]
    ).astype(jnp.int32)
    meta = jnp.stack([pick(jnp.ones_like(place)), pick(place % NEIGH), pick((lists % per_owner)[None])], axis=1)
    vec = jnp.pad(jnp.repeat(meta.astype(F32), BLOCK, axis=2), ((0, 0), (0, 5), (0, 0)))
    cnt = jnp.broadcast_to(counts.astype(F32)[:, None, None], (blocks, 8, NY * BLOCK))

    lanes = NY * BLOCK
    vm = pltpu.VMEM
    scratch = [
        vm((2 * NX, tok, 1024), BF16),
        vm((2 * NX, width, 1024), BF16),
        vm((2, tok // 2, width), F32),
        vm((2, OWN, 256, width), BF16),
        vm((RDR * blocks, BLOCK, width), BF16),
        vm((RDR * blocks, BLOCK, width), BF16),
        vm((RDR * blocks, 8, lanes), F32),
        vm((OWN, lanes, width), BF16),
        vm((OWN, lanes, width), BF16),
        vm((OWN, heads, 128, lanes), F32),
        vm((OWN, heads, 128, lanes), F32),
        vm((NY * OWN, 8, lanes), F32),
        vm((NY * OWN, 8, lanes), F32),
        vm((OWN, 8, lanes), F32),
        vm((OWN * RDR, BLOCK, width), BF16),
        vm((2, OWN, 256, width), BF16),
        vm((2, 4, 256, width), BF16),
        vm((2, 4, 256, width), BF16),
        vm((RDR * blocks, BLOCK, width), BF16),
        vm((12, BLOCK, width), BF16),
        vm((12, BLOCK, width), BF16),
        pltpu.SemaphoreType.DMA((MAX_COPIES,)),
        pltpu.SemaphoreType.DMA((MAX_COPIES,)),
        pltpu.SemaphoreType.DMA((16,)),
    ]
    hbm = pl.BlockSpec(memory_space=pl.ANY)
    vmem = pl.BlockSpec(memory_space=pltpu.VMEM)
    smem = pl.BlockSpec(memory_space=pltpu.SMEM)
    dq, dk, dv = pl.pallas_call(
        functools.partial(body, heads),
        out_shape=(
            jax.ShapeDtypeStruct((blocks, BLOCK, width), BF16),
            jax.ShapeDtypeStruct((256, width), BF16),
            jax.ShapeDtypeStruct((256, width), BF16),
        ),
        in_specs=[smem, vmem, hbm, hbm, hbm, hbm, hbm, hbm],
        out_specs=(vmem, vmem, vmem),
        scratch_shapes=scratch,
        compiler_params=pltpu.CompilerParams(
            collective_id=0, has_side_effects=True, vmem_limit_bytes=63 * 1024 * 1024
        ),
        name="column_attention_grad",
    )(
        scal,
        vec,
        cnt,
        out_grad,
        out_weight,
        queries.reshape(blocks, BLOCK, width),
        keys.reshape(256, width),
        values.reshape(256, width),
    )
    return dq.reshape(tok, width), dk.reshape(keys.shape), dv.reshape(values.shape)


def solution(mesh):
    return jax.shard_map(
        on_device,
        mesh=mesh,
        in_specs=(
            P("seq", "mp"),
            P("mp", None),
            P("seq", "mp"),
            P("seq", None, "mp"),
            P("seq", None, "mp"),
            P(),
            P("seq"),
        ),
        out_specs=(P("seq", "mp"), P("seq", None, "mp"), P("seq", None, "mp")),
        check_vma=False,
    )
```

```python
import functools
import math

import jax
import jax.numpy as jnp
from jax import lax
from jax.experimental import pallas as pl
from jax.experimental.pallas import tpu as pltpu
from jax.sharding import PartitionSpec as P

HEAD = 128
BLOCK = 64
NEIGH = 2
NX, NY, NZ = 4, 4, 8
OWN = NZ
RDR = NY
LOW = -1e30
MESH = pl.DeviceIdType.MESH
F32, BF16 = jnp.float32, jnp.bfloat16
NT = (((1,), (1,)), ((), ()))
NN = (((1,), (0,)), ((), ()))
TN = (((0,), (0,)), ((), ()))


class Ids:
    def __init__(self):
        self.at = {}

    def __call__(self, *name):
        return self.at.setdefault(name, len(self.at))


MAX_COPIES = 120
LOCAL_IN = 12
BLK, OTHER, PAIR, MINE, EXISTS, PLACE, PARITY = 0, 32, 64, 128, 192, 224, 256


def body(
    heads,
    ret,
    cnt_in,
    og_in,
    w_in,
    q_in,
    k_in,
    v_in,
    dq_out,
    dkv_out,
    og,
    w,
    acc,
    kv,
    q_all,
    do_all,
    cnt_all,
    q_own,
    do_own,
    ex,
    gw,
    st1,
    st2,
    fac,
    dqp,
    dkv,
    rsr,
    rsl,
    dqb,
    dq_far,
    scal,
    ssem,
    rsem,
    lsem,
):
    ids = Ids()
    scale = 1.0 / math.sqrt(HEAD)
    seq, mp = lax.axis_index("seq"), lax.axis_index("mp")
    y, z = seq // NZ, seq % NZ
    x, core = mp // 2, mp % 2
    part = BLOCK * 2

    def at_x(d):
        return (seq, ((x + d) % NX) * 2 + core)

    sibling = (seq, x * 2 + (1 - core))

    def at_y(d):
        return (((y + d) % NY) * NZ + z, mp)

    def at_z(d):
        return (y * NZ + (z + d) % NZ, mp)

    def zz(d):
        return (z + d) % NZ

    started = []

    def send(name, src, dst, dev):
        i = ids(*name)
        cp = pltpu.make_async_remote_copy(
            src_ref=src, dst_ref=dst, send_sem=ssem.at[i], recv_sem=rsem.at[i], device_id=dev, device_id_type=MESH
        )
        cp.start()
        started.append(cp)

    def recv(name, dst):
        i = ids(*name)
        pltpu.make_async_remote_copy(
            src_ref=dst, dst_ref=dst, send_sem=ssem.at[i], recv_sem=rsem.at[i], device_id=sibling, device_id_type=MESH
        ).wait_recv()

    barrier = pltpu.get_barrier_semaphore()
    peers = [at_x(1), at_x(-1), sibling, at_y(1), at_y(-1), at_y(2), at_z(1), at_z(-1)]
    for dev in peers:
        pl.semaphore_signal(barrier, inc=1, device_id=dev, device_id_type=MESH)

    local = []

    def local_copy(src, dst):
        cp = pltpu.make_async_copy(src, dst, lsem.at[len(local)])
        cp.start()
        local.append(cp)

    local_copy(og_in, og.at[mp])
    for c in range(2 * NX):
        local_copy(w_in.at[:, pl.ds(c * 1024, 1024)], w.at[c])
    local_copy(q_in, q_all.at[pl.ds(y * 8, 8)])
    local_copy(k_in, kv.at[0, z])
    local_copy(v_in, kv.at[1, z])

    def tables(r, carry):
        base = (r * NZ + z) * 8
        named = [ret[j % 2, base + j // 2] for j in range(16)]
        owner = [e >> 1 for e in named]
        code = []
        for j in range(16):
            own = owner[j] - y * OWN
            near = (own >= 0) & (own < OWN)
            scal[PAIR + r * 16 + j] = jnp.where(near, own, 0) * RDR + r
            scal[MINE + r * 16 + j] = jnp.where(near, 1, 0)
            code.append((owner[j ^ 1] << 5) + ((named[j] & 1) << 4) + ((j % 2) << 3) + j // 2 + 1024)
        for o in range(OWN):
            t = 0
            for j in range(16):
                t = t + jnp.where(owner[j] == y * OWN + o, code[j], 0)
            scal[BLK + o * RDR + r] = r * 8 + (t & 7)
            scal[PLACE + o * RDR + r] = (t >> 3) & 1
            scal[PARITY + o * RDR + r] = (t >> 4) & 1
            scal[OTHER + o * RDR + r] = (t >> 5) & 31
            scal[EXISTS + o * RDR + r] = t >> 10
        return carry

    for b in range(8):
        cnt_all[y * 8 + b] = jnp.full((8, RDR * BLOCK), cnt_in[b].astype(F32))

    pl.semaphore_wait(barrier, len(peers))

    def kv_piece(a, o, e):
        return kv.at[a, o, pl.ds(e * 128, 128)]

    pieces = [(a, e) for a in range(2) for e in range(2)]

    def kv_first():
        for a, e in pieces:
            src = (k_in, v_in)[a].at[pl.ds(e * 128, 128)]
            send(("kvR", 1, a, e), src, kv_piece(a, z, e), at_z(1))
            send(("kvL", 1, a, e), src, kv_piece(a, z, e), at_z(-1))

    def kv_hop(k):
        for a, e in pieces:
            if k < 4 or e == 0:
                o = zz(-k)
                recv(("kvR", k, a, e), kv_piece(a, o, e))
                if k < 3 or (k == 3 and e == 0):
                    send(("kvR", k + 1, a, e), kv_piece(a, o, e), kv_piece(a, o, e), at_z(1))
            if k < 4 or e == 1:
                o = zz(k)
                recv(("kvL", k, a, e), kv_piece(a, o, e))
                if k < 3 or (k == 3 and e == 1):
                    send(("kvL", k + 1, a, e), kv_piece(a, o, e), kv_piece(a, o, e), at_z(-1))

    def y_rows(d, h, n=4):
        return pl.ds(((y + d) % NY) * 8 + h * n, n)

    def y_first(tag, src, buf, h, n, way):
        send((tag, way, h), src, buf.at[y_rows(0, h, n)], at_y(1 if way == "R" else -1))

    def y_on(tag, buf, h, n):
        even = h % 2 == 0
        rows = buf.at[y_rows(-1 if even else 1, h, n)]
        recv((tag, "R" if even else "L", h), rows)
        send((tag, "F", h), rows, rows, at_y(1 if even else -1))

    def y_rest(tag, buf, h, n):
        even = h % 2 == 0
        recv((tag, "L" if even else "R", h), buf.at[y_rows(1 if even else -1, h, n)])
        recv((tag, "F", h), buf.at[y_rows(2, h, n)])

    def y_direct(tag, src, buf, rows):
        mine = buf.at[pl.ds(y * rows, rows)]
        for d in (1, -1, 2):
            send((tag, d), src if src is not None else mine, mine, at_y(d))

    def y_direct_wait(tag, buf, rows):
        for d in (1, -1, 2):
            recv((tag, d), buf.at[pl.ds(((y - d) % NY) * rows, rows)])

    def og_piece(d, t, other=False):
        c = ((x + d) % NX) * 2 + ((1 - core) if other else core)
        return og.at[c, pl.ds(t * part, part)]

    def x_own(t, way):
        src = og_in.at[pl.ds(t * part, part)]
        send(("og", way, t), src, og_piece(0, t), at_x(1 if way == "R" else -1))

    def x_pass(d, t):
        piece = og_piece(d, t)
        recv(("og", {-1: "R", 1: "L", 2: "F"}[d], t), piece)
        if d == (-1 if t % 2 == 0 else 1):
            send(("og", "F", t), piece, piece, at_x(-d))
        send(("ogc", d, t), piece, piece, sibling)

    def mm(d, t, n=1):
        rows = pl.ds(t * part, n * part)
        for other in (False, True):
            c = ((x + d) % NX) * 2 + ((1 - core) if other else core)
            if other and d == 0:
                recv(("ogc", 0), og.at[c])
            elif other:
                for i in range(t, t + n):
                    recv(("ogc", d, i), og_piece(d, i, True))
            p = lax.dot_general(og[c, rows, :], w[c], NT, preferred_element_type=F32)
            if d == 0 and not other:
                acc[rows, :] = p
            else:
                acc[rows, :] += p

    def grad_done(t):
        do_all[y_rows(0, t, 2)] = acc[pl.ds(t * part, part), :].astype(BF16).reshape(2, BLOCK, heads * HEAD)
        src = do_all.at[y_rows(0, t, 2)]
        for way in ("R", "L"):
            y_first("do", src, do_all, t, 2, way)

    lane_reader = lax.broadcasted_iota(jnp.int32, (8, RDR * BLOCK), 1) // BLOCK

    def lane_pick(base, o):
        t = jnp.full((8, RDR * BLOCK), scal[base + o * RDR])
        for r in range(1, RDR):
            t = jnp.where(lane_reader == r, scal[base + o * RDR + r], t)
        return t.astype(F32)[0:1]

    def gather_blocks(src, dst, o):
        for r in range(RDR):
            dst[o, pl.ds(r * BLOCK, BLOCK), :] = src[scal[BLK + o * RDR + r]]

    def partner_rows(buf, o, base):
        t = buf[scal[base + o * RDR]]
        for r in range(1, RDR):
            t = jnp.where(lane_reader == r, buf[scal[base + o * RDR + r]], t)
        return t

    def cols(h):
        return pl.ds(h * HEAD, HEAD)

    def score_one(o):
        gather_blocks(q_all, q_own, o)
        par = lane_pick(PARITY, o)
        for h in range(heads):
            s = lax.dot_general(kv[0, o, :, cols(h)], q_own[o, :, cols(h)], NT, preferred_element_type=F32)
            s = jnp.where(par > 0.5, s[128:], s[:128]) * scale
            m = jnp.max(s, axis=0, keepdims=True)
            e = jnp.exp(s - m)
            ex[o, h] = e
            st1[y * OWN + o, h : h + 1, :] = m
            st1[y * OWN + o, heads + h : heads + h + 1, :] = jnp.sum(e, axis=0, keepdims=True)

    def scores(dist):
        if dist in (0, 4):
            score_one(zz(dist))
        else:

            def one(i, carry):
                score_one(zz(dist * (1 - 2 * i)))
                return carry

            lax.fori_loop(0, 2, one, 0)

    def lives(o):
        exists, place = lane_pick(EXISTS, o), lane_pick(PLACE, o)
        short = 2.0 - partner_rows(cnt_all, o, BLK)[0:1, :]
        return exists * (1.0 - place * short) > 0.5, exists * (1.0 - (1.0 - place) * short) > 0.5

    def factors():
        def one(o, carry):
            live, live_p = lives(o)
            own = st1[y * OWN + o]
            oth = partner_rows(st1, o, OTHER)
            m_o, l_o = own[:heads], own[heads : 2 * heads]
            m_p = jnp.where(live_p, oth[:heads], LOW)
            l_p = jnp.where(live_p, oth[heads : 2 * heads], 0.0)
            m = jnp.maximum(m_o, m_p)
            a = jnp.exp(m_o - m)
            f = jnp.where(live, a / (l_o * a + l_p * jnp.exp(m_p - m)), 0.0)
            par = lane_pick(PARITY, o)
            fac[o, 0:heads, :] = f * (1.0 - par)
            fac[o, heads : 2 * heads, :] = f * par
            return carry

        lax.fori_loop(0, OWN, one, 0)

    def both(o, h, t0, t1):
        return jnp.concatenate([t0.astype(BF16), t1.astype(BF16)], axis=0)

    def value_one(o):
        gather_blocks(do_all, do_own, o)
        for h in range(heads):
            e = ex[o, h]
            p = both(o, h, e * fac[o, h : h + 1, :], e * fac[o, heads + h : heads + h + 1, :])
            t = lax.dot_general(p, do_own[o, :, cols(h)], NN, preferred_element_type=F32)
            dkv[1, o, :, cols(h)] = t.astype(BF16)

    def dots_one(o):
        par = lane_pick(PARITY, o)
        for h in range(heads):
            g = lax.dot_general(kv[1, o, :, cols(h)], do_own[o, :, cols(h)], NT, preferred_element_type=F32)
            g = jnp.where(par > 0.5, g[128:], g[:128])
            gw[o, h] = g
            f = fac[o, h : h + 1, :] + fac[o, heads + h : heads + h + 1, :]
            p = (ex[o, h] * f).astype(BF16).astype(F32)
            st2[y * OWN + o, h : h + 1, :] = jnp.sum(p * g, axis=0, keepdims=True)

    def key_one(o):
        _, live_p = lives(o)
        rd = st2[y * OWN + o][:heads] + jnp.where(live_p, partner_rows(st2, o, OTHER)[:heads], 0.0)
        for h in range(heads):
            e = ex[o, h]
            t = gw[o, h] - rd[h : h + 1]
            d = both(o, h, e * fac[o, h : h + 1, :] * t, e * fac[o, heads + h : heads + h + 1, :] * t)
            dk = lax.dot_general(d, q_own[o, :, cols(h)], NN, preferred_element_type=F32)
            dkv[0, o, :, cols(h)] = (dk * scale).astype(BF16)
            dq = lax.dot_general(d, kv[0, o, :, cols(h)], TN, preferred_element_type=F32)
            dqp[pl.ds(o * RDR, RDR), :, cols(h)] = (dq * scale).astype(BF16).reshape(RDR, BLOCK, HEAD)

    def per_owner(fn, dist):
        if dist in (0, 4):
            fn(zz(dist))
        else:

            def one(i, carry):
                fn(zz(dist * (1 - 2 * i)))
                return carry

            lax.fori_loop(0, 2, one, 0)

    def rs_buf(way, a, k, e):
        rows = pl.ds(e * 128, 128)
        if k == 3:
            return dkv_out.at[a, 1 if way == "R" else 2, rows]
        return (rsr if way == "R" else rsl).at[a, k, rows]

    def rs_hop(way, a, k, e):
        far = 0 if way == "R" else 1
        sign = 1 if way == "R" else -1
        o = zz(sign * (4 - k))
        piece = dkv.at[a, o, pl.ds(e * 128, 128)]
        if k > 1 or (k == 1 and e == far):
            rs_take(way, a, k - 1, e, o)
        send(("rs" + way, a, k, e), piece, rs_buf(way, a, k, e), at_z(sign))

    def rs_take(way, a, k, e, o):
        buf = rsr if way == "R" else rsl
        recv(("rs" + way, a, k, e), rs_buf(way, a, k, e))
        rows = pl.ds(e * 128, 128)
        dkv[a, o, rows, :] = (dkv[a, o, rows, :].astype(F32) + buf[a, k, rows, :].astype(F32)).astype(BF16)

    def rs_round(a, k):
        for e in range(2):
            for way, far in (("R", 0), ("L", 1)):
                if k > 0 or e == far:
                    rs_hop(way, a, k, e)

    kv_first()
    for t in range(3):
        x_own(t, "R")
        x_own(t, "L")
    for h in range(2):
        src = q_in.at[pl.ds(h * 4, 4)], q_in.at[pl.ds(4 - h * 4, 4)]
        y_first("q", src[0], q_all, h, 4, "R")
        y_first("q", src[1], q_all, 1 - h, 4, "L")
    send(("ogc", 0), og_in, og.at[mp], sibling)
    y_direct("cnt", None, cnt_all, 8)
    lax.fori_loop(0, RDR, tables, 0)

    for h in range(2):
        y_on("q", q_all, h, 4)
    x_pass(-1, 0)
    x_pass(1, 0)
    x_own(3, "L")
    kv_hop(1)
    x_pass(-1, 1)
    x_pass(1, 1)
    for cp in local:
        cp.wait()
    mm(0, 0, 4)
    for h in range(2):
        y_rest("q", q_all, h, 4)
    y_direct_wait("cnt", cnt_all, 8)
    scores(0)
    x_pass(-1, 2)
    x_own(3, "R")
    x_pass(1, 2)
    scores(1)
    mm(-1, 0, 3)
    mm(1, 0, 3)

    kv_hop(2)
    x_pass(2, 0)
    x_pass(1, 3)
    mm(2, 0)
    grad_done(0)
    mm(1, 3)
    scores(2)

    x_pass(2, 1)
    x_pass(2, 2)
    mm(2, 1, 2)
    grad_done(1)
    grad_done(2)
    y_on("do", do_all, 0, 2)
    kv_hop(3)
    x_pass(-1, 3)
    x_pass(2, 3)
    mm(-1, 3)
    mm(2, 3)
    grad_done(3)
    for t in (1, 2):
        y_on("do", do_all, t, 2)
    scores(3)
    kv_hop(4)
    y_on("do", do_all, 3, 2)
    scores(4)
    y_direct("st1", None, st1, OWN)
    for t in range(3):
        y_rest("do", do_all, t, 2)
    y_direct_wait("st1", st1, OWN)
    factors()
    y_rest("do", do_all, 3, 2)

    per_owner(value_one, 4)
    rs_round(1, 0)
    per_owner(value_one, 3)
    rs_hop("R", 1, 1, 1)
    rs_hop("L", 1, 1, 0)
    for d in (2, 1, 0):
        per_owner(value_one, d)
    for d in (4, 3):
        per_owner(dots_one, d)
    rs_hop("R", 1, 1, 0)
    rs_hop("L", 1, 1, 1)
    for d in (2, 1, 0):
        per_owner(dots_one, d)
    y_direct("st2", None, st2, OWN)
    rs_round(1, 2)
    y_direct_wait("st2", st2, OWN)

    per_owner(key_one, 4)
    rs_round(0, 0)
    per_owner(key_one, 3)
    rs_hop("R", 0, 1, 1)
    rs_hop("L", 0, 1, 0)
    per_owner(key_one, 2)
    rs_round(1, 3)
    rs_hop("R", 0, 1, 0)
    rs_hop("L", 0, 1, 1)
    for d in (1, 0):
        per_owner(key_one, d)
    for a in range(2):
        local_copy(dkv.at[a, z], dkv_out.at[a, 0])

    def blocks(r, carry):
        def one(b, carry2):
            j = r * 16 + b * 2
            t = dqp[scal[PAIR + j]].astype(F32) * scal[MINE + j].astype(F32)
            t += dqp[scal[PAIR + 1 + j]].astype(F32) * scal[MINE + 1 + j].astype(F32)
            dqb[r * 8 + b] = t.astype(BF16)
            return carry2

        return lax.fori_loop(0, 8, one, carry)

    lax.fori_loop(0, RDR, blocks, 0)

    def dq_rows(d, h):
        return dqb.at[y_rows(d, h)]

    def dq_land(way, h):
        return dq_out.at[1 if way == "R" else 2, pl.ds(h * 4, 4)]

    send(("dq", "R", "far"), dq_rows(2, 0), dq_far.at[pl.ds(0, 4)], at_y(1))
    send(("dq", "L", "far"), dq_rows(2, 1), dq_far.at[pl.ds(4, 4)], at_y(-1))
    send(("dq", "R", 1), dq_rows(1, 1), dq_land("R", 1), at_y(1))
    send(("dq", "L", 0), dq_rows(-1, 0), dq_land("L", 0), at_y(-1))
    local_copy(dqb.at[pl.ds(y * 8, 8)], dq_out.at[0])

    rs_round(0, 2)

    def dq_on(way, h, d):
        far = pl.ds(h * 4, 4)
        recv(("dq", way, "far"), dq_far.at[far])
        rows = y_rows(d, h)
        dqb[rows] = (dqb[rows].astype(F32) + dq_far[far].astype(F32)).astype(BF16)
        send(("dq", way, h), dqb.at[rows], dq_land(way, h), at_y(d))

    dq_on("R", 0, 1)
    dq_on("L", 1, -1)

    def rs_last(a):
        for e in range(2):
            for way in ("R", "L"):
                recv(("rs" + way, a, 3, e), rs_buf(way, a, 3, e))

    rs_round(0, 3)
    for cp in local[LOCAL_IN:]:
        cp.wait()
    rs_last(1)
    for h in range(2):
        for way in ("R", "L"):
            recv(("dq", way, h), dq_land(way, h))
    rs_last(0)
    for cp in started:
        cp.wait_send()


def sums(dq_in, dkv_in, dq_out, dk_out, dv_out):
    def three(t):
        return (t[0].astype(F32) + t[1].astype(F32) + t[2].astype(F32)).astype(BF16)

    for b in range(8):
        dq_out[pl.ds(b * BLOCK, BLOCK), :] = three(dq_in[:, b])
    for out, a in ((dk_out, 0), (dv_out, 1)):
        for e in range(2):
            out[e] = three(dkv_in[a, :, pl.ds(e * 128, 128), :])


def on_device(out_grad, out_weight, queries, keys, values, retrieval, counts):
    tok, width = queries.shape
    heads = width // HEAD
    blocks = tok // BLOCK
    lanes = NY * BLOCK
    vm = pltpu.VMEM
    scratch = [
        vm((2 * NX, tok, 1024), BF16),
        vm((2 * NX, width, 1024), BF16),
        vm((tok, width), F32),
        vm((2, OWN, 256, width), BF16),
        vm((RDR * blocks, BLOCK, width), BF16),
        vm((RDR * blocks, BLOCK, width), BF16),
        vm((RDR * blocks, 8, lanes), F32),
        vm((OWN, lanes, width), BF16),
        vm((OWN, lanes, width), BF16),
        vm((OWN, heads, 128, lanes), F32),
        vm((OWN, heads, 128, lanes), F32),
        vm((NY * OWN, 8, lanes), F32),
        vm((NY * OWN, 8, lanes), F32),
        vm((OWN, 8, lanes), F32),
        vm((OWN * RDR, BLOCK, width), BF16),
        vm((2, OWN, 256, width), BF16),
        vm((2, 3, 256, width), BF16),
        vm((2, 3, 256, width), BF16),
        vm((RDR * blocks, BLOCK, width), BF16),
        vm((8, BLOCK, width), BF16),
        pltpu.SMEM((288,), jnp.int32),
        pltpu.SemaphoreType.DMA((MAX_COPIES,)),
        pltpu.SemaphoreType.DMA((MAX_COPIES,)),
        pltpu.SemaphoreType.DMA((16,)),
    ]
    hbm = pl.BlockSpec(memory_space=pl.ANY)
    vmem = pl.BlockSpec(memory_space=pltpu.VMEM)
    smem = pl.BlockSpec(memory_space=pltpu.SMEM)
    dq_parts, dkv_parts = pl.pallas_call(
        functools.partial(body, heads),
        out_shape=(
            jax.ShapeDtypeStruct((3, blocks, BLOCK, width), BF16),
            jax.ShapeDtypeStruct((2, 3, 256, width), BF16),
        ),
        in_specs=[smem, smem, hbm, hbm, hbm, hbm, hbm],
        out_specs=(hbm, hbm),
        scratch_shapes=scratch,
        compiler_params=pltpu.CompilerParams(
            collective_id=0, has_side_effects=True, vmem_limit_bytes=63 * 1024 * 1024
        ),
        name="column_attention_grad",
    )(
        retrieval.T,
        counts,
        out_grad,
        out_weight,
        queries.reshape(blocks, BLOCK, width),
        keys.reshape(256, width),
        values.reshape(256, width),
    )
    return pl.pallas_call(
        sums,
        out_shape=(
            jax.ShapeDtypeStruct(queries.shape, BF16),
            jax.ShapeDtypeStruct(keys.shape, BF16),
            jax.ShapeDtypeStruct(values.shape, BF16),
        ),
        in_specs=[vmem, vmem],
        out_specs=(vmem, vmem, vmem),
        name="sums_of_sides",
    )(dq_parts, dkv_parts)


def solution(mesh):
    return jax.shard_map(
        on_device,
        mesh=mesh,
        in_specs=(
            P("seq", "mp"),
            P("mp", None),
            P("seq", "mp"),
            P("seq", None, "mp"),
            P("seq", None, "mp"),
            P(),
            P("seq"),
        ),
        out_specs=(P("seq", "mp"), P("seq", None, "mp"), P("seq", None, "mp")),
        check_vma=False,
    )
```

```python
import functools
import math

import jax
import jax.numpy as jnp
from jax import lax
from jax.experimental import pallas as pl
from jax.experimental.pallas import tpu as pltpu
from jax.sharding import PartitionSpec as P

HEAD = 128
BLOCK = 64
NEIGH = 2
NX, NY, NZ = 4, 4, 8
OWN = NZ
RDR = NY
LOW = -1e30
MESH = pl.DeviceIdType.MESH
F32, BF16 = jnp.float32, jnp.bfloat16
NT = (((1,), (1,)), ((), ()))
NN = (((1,), (0,)), ((), ()))
TN = (((0,), (0,)), ((), ()))


class Ids:
    def __init__(self):
        self.at = {}

    def __call__(self, *name):
        return self.at.setdefault(name, len(self.at))


MAX_COPIES = 144
GROUPS = ((0, 0, 2), (1, 2, 2), (2, 4, 2), (3, 6, 1), (4, 7, 1))
HALVES = ((0, 0, 4), (1, 4, 4))
LOCAL_IN = 12
BLK, OTHER, PAIR, MINE, EXISTS, PLACE, PARITY = 0, 32, 64, 128, 192, 224, 256


def body(
    heads,
    ret,
    cnt_in,
    og_in,
    w_in,
    q_in,
    k_in,
    v_in,
    dq_out,
    dkv_out,
    og,
    w,
    acc,
    kv,
    q_all,
    do_all,
    cnt_all,
    q_own,
    do_own,
    ex,
    gw,
    st1,
    st2,
    fac,
    dqp,
    dkv,
    rsr,
    rsl,
    dqb,
    dq_far,
    scal,
    ssem,
    rsem,
    lsem,
):
    ids = Ids()
    scale = 1.0 / math.sqrt(HEAD)
    seq, mp = lax.axis_index("seq"), lax.axis_index("mp")
    y, z = seq // NZ, seq % NZ
    x, core = mp // 2, mp % 2

    def at_x(d):
        return (seq, ((x + d) % NX) * 2 + core)

    sibling = (seq, x * 2 + (1 - core))

    def at_y(d):
        return (((y + d) % NY) * NZ + z, mp)

    def at_z(d):
        return (y * NZ + (z + d) % NZ, mp)

    def zz(d):
        return (z + d) % NZ

    started = []

    def send(name, src, dst, dev):
        i = ids(*name)
        cp = pltpu.make_async_remote_copy(
            src_ref=src, dst_ref=dst, send_sem=ssem.at[i], recv_sem=rsem.at[i], device_id=dev, device_id_type=MESH
        )
        cp.start()
        started.append(cp)

    def recv(name, dst):
        i = ids(*name)
        pltpu.make_async_remote_copy(
            src_ref=dst, dst_ref=dst, send_sem=ssem.at[i], recv_sem=rsem.at[i], device_id=sibling, device_id_type=MESH
        ).wait_recv()

    barrier = pltpu.get_barrier_semaphore()
    peers = [at_x(1), at_x(-1), sibling, at_y(1), at_y(-1), at_y(2), at_z(1), at_z(-1)]
    for dev in peers:
        pl.semaphore_signal(barrier, inc=1, device_id=dev, device_id_type=MESH)

    local = []

    def local_copy(src, dst):
        cp = pltpu.make_async_copy(src, dst, lsem.at[len(local)])
        cp.start()
        local.append(cp)

    local_copy(og_in, og.at[mp])
    for c in range(2 * NX):
        local_copy(w_in.at[:, pl.ds(c * 1024, 1024)], w.at[c])
    local_copy(q_in, q_all.at[pl.ds(y * 8, 8)])
    local_copy(k_in, kv.at[0, z])
    local_copy(v_in, kv.at[1, z])

    def tables(r, carry):
        base = (r * NZ + z) * 8
        named = [ret[j % 2, base + j // 2] for j in range(16)]
        owner = [e >> 1 for e in named]
        code = []
        for j in range(16):
            own = owner[j] - y * OWN
            near = (own >= 0) & (own < OWN)
            scal[PAIR + r * 16 + j] = jnp.where(near, own, 0) * RDR + r
            scal[MINE + r * 16 + j] = jnp.where(near, 1, 0)
            code.append((owner[j ^ 1] << 5) + ((named[j] & 1) << 4) + ((j % 2) << 3) + j // 2 + 1024)
        for o in range(OWN):
            t = 0
            for j in range(16):
                t = t + jnp.where(owner[j] == y * OWN + o, code[j], 0)
            scal[BLK + o * RDR + r] = r * 8 + (t & 7)
            scal[PLACE + o * RDR + r] = (t >> 3) & 1
            scal[PARITY + o * RDR + r] = (t >> 4) & 1
            scal[OTHER + o * RDR + r] = (t >> 5) & 31
            scal[EXISTS + o * RDR + r] = t >> 10
        return carry

    for b in range(8):
        cnt_all[y * 8 + b] = jnp.full((8, RDR * BLOCK), cnt_in[b].astype(F32))

    pl.semaphore_wait(barrier, len(peers))

    def kv_piece(a, o, e):
        return kv.at[a, o, pl.ds(e * 128, 128)]

    pieces = [(a, e) for a in range(2) for e in range(2)]

    def kv_first():
        for a, e in pieces:
            src = (k_in, v_in)[a].at[pl.ds(e * 128, 128)]
            send(("kvR", 1, a, e), src, kv_piece(a, z, e), at_z(1))
            send(("kvL", 1, a, e), src, kv_piece(a, z, e), at_z(-1))

    def kv_hop(k, a):
        for e in range(2):
            if k < 4 or e == 0:
                o = zz(-k)
                recv(("kvR", k, a, e), kv_piece(a, o, e))
                if k < 3 or (k == 3 and e == 0):
                    send(("kvR", k + 1, a, e), kv_piece(a, o, e), kv_piece(a, o, e), at_z(1))
            if k < 4 or e == 1:
                o = zz(k)
                recv(("kvL", k, a, e), kv_piece(a, o, e))
                if k < 3 or (k == 3 and e == 1):
                    send(("kvL", k + 1, a, e), kv_piece(a, o, e), kv_piece(a, o, e), at_z(-1))

    def y_rows(d, part):
        return pl.ds(((y + d) % NY) * 8 + part[1], part[2])

    def y_first(tag, src, buf, part, way):
        send((tag, way, part[0]), src, buf.at[y_rows(0, part)], at_y(1 if way == "R" else -1))

    def y_on(tag, buf, part):
        even = part[0] % 2 == 0
        rows = buf.at[y_rows(-1 if even else 1, part)]
        recv((tag, "R" if even else "L", part[0]), rows)
        send((tag, "F", part[0]), rows, rows, at_y(1 if even else -1))

    def y_rest(tag, buf, part):
        even = part[0] % 2 == 0
        recv((tag, "L" if even else "R", part[0]), buf.at[y_rows(1 if even else -1, part)])
        recv((tag, "F", part[0]), buf.at[y_rows(2, part)])

    def y_direct(tag, src, buf, rows):
        mine = buf.at[pl.ds(y * rows, rows)]
        for d in (1, -1, 2):
            send((tag, d), src if src is not None else mine, mine, at_y(d))

    def y_direct_wait(tag, buf, rows):
        for d in (1, -1, 2):
            recv((tag, d), buf.at[pl.ds(((y - d) % NY) * rows, rows)])

    def og_piece(d, g, i=None, other=False):
        c = ((x + d) % NX) * 2 + ((1 - core) if other else core)
        return og.at[c, og_rows(g, i)]

    def og_rows(g, i=None):
        _, b0, n = GROUPS[g]
        if i is None:
            return pl.ds(b0 * BLOCK, n * BLOCK)
        return pl.ds(b0 * BLOCK + i * (n * BLOCK // 2), n * BLOCK // 2)

    def x_own(way, g, i):
        if g < len(GROUPS):
            send(("og", way, g, i), og_in.at[og_rows(g, i)], og_piece(0, g, i), at_x(1 if way == "R" else -1))

    def x_start():
        for n in range(3):
            x_own("R", n // 2, n % 2)
            x_own("L", n // 2, 1 - n % 2)

    def x_on(g):
        for way, i, d in (("R", 0, -1), ("L", 1, 1)):
            piece = og_piece(d, g, i)
            recv(("og", way, g, i), piece)
            send(("og", "F", g, i), piece, piece, at_x(-d))
            x_own(way, g + 1, 1 - i)
            x_own(way, g + 2, i)

    def x_near(g):
        for way, i, d in (("R", 1, -1), ("L", 0, 1)):
            recv(("og", way, g, i), og_piece(d, g, i))
            piece = og_piece(d, g)
            send(("ogc", d, g), piece, piece, sibling)

    def x_far(g):
        for i in range(2):
            recv(("og", "F", g, i), og_piece(2, g, i))
        piece = og_piece(2, g)
        send(("ogc", 2, g), piece, piece, sibling)

    def mm_own():
        for c in (mp, x * 2 + 1 - core):
            p = lax.dot_general(og[c], w[c], NT, preferred_element_type=F32)
            if c is mp:
                acc[...] = p
                recv(("ogc", 0), og.at[x * 2 + 1 - core])
            else:
                acc[...] += p

    def mm(d, g):
        rows = og_rows(g)
        for other in (False, True):
            c = ((x + d) % NX) * 2 + ((1 - core) if other else core)
            if other:
                recv(("ogc", d, g), og_piece(d, g, None, True))
            acc[rows, :] += lax.dot_general(og[c, rows, :], w[c], NT, preferred_element_type=F32)

    def grad_done(g):
        n = GROUPS[g][2]
        do_all[y_rows(0, GROUPS[g])] = acc[og_rows(g), :].astype(BF16).reshape(n, BLOCK, heads * HEAD)
        src = do_all.at[y_rows(0, GROUPS[g])]
        for way in ("R", "L"):
            y_first("do", src, do_all, GROUPS[g], way)

    def do_on(g):
        y_on("do", do_all, GROUPS[g])

    lane_reader = lax.broadcasted_iota(jnp.int32, (8, RDR * BLOCK), 1) // BLOCK

    def lane_pick(base, o):
        t = jnp.full((8, RDR * BLOCK), scal[base + o * RDR])
        for r in range(1, RDR):
            t = jnp.where(lane_reader == r, scal[base + o * RDR + r], t)
        return t.astype(F32)[0:1]

    def gather_blocks(src, dst, o):
        for r in range(RDR):
            dst[o, pl.ds(r * BLOCK, BLOCK), :] = src[scal[BLK + o * RDR + r]]

    def partner_rows(buf, o, base):
        t = buf[scal[base + o * RDR]]
        for r in range(1, RDR):
            t = jnp.where(lane_reader == r, buf[scal[base + o * RDR + r]], t)
        return t

    def cols(h):
        return pl.ds(h * HEAD, HEAD)

    def score_one(o):
        gather_blocks(q_all, q_own, o)
        par = lane_pick(PARITY, o)
        for h in range(heads):
            s = lax.dot_general(kv[0, o, :, cols(h)], q_own[o, :, cols(h)], NT, preferred_element_type=F32)
            s = jnp.where(par > 0.5, s[128:], s[:128]) * scale
            m = jnp.max(s, axis=0, keepdims=True)
            e = jnp.exp(s - m)
            ex[o, h] = e
            st1[y * OWN + o, h : h + 1, :] = m
            st1[y * OWN + o, heads + h : heads + h + 1, :] = jnp.sum(e, axis=0, keepdims=True)

    def scores(dist):
        if dist in (0, 4):
            score_one(zz(dist))
        else:

            def one(i, carry):
                score_one(zz(dist * (1 - 2 * i)))
                return carry

            lax.fori_loop(0, 2, one, 0)

    def lives(o):
        exists, place = lane_pick(EXISTS, o), lane_pick(PLACE, o)
        short = 2.0 - partner_rows(cnt_all, o, BLK)[0:1, :]
        return exists * (1.0 - place * short) > 0.5, exists * (1.0 - (1.0 - place) * short) > 0.5

    def factors():
        def one(o, carry):
            live, live_p = lives(o)
            own = st1[y * OWN + o]
            oth = partner_rows(st1, o, OTHER)
            m_o, l_o = own[:heads], own[heads : 2 * heads]
            m_p = jnp.where(live_p, oth[:heads], LOW)
            l_p = jnp.where(live_p, oth[heads : 2 * heads], 0.0)
            m = jnp.maximum(m_o, m_p)
            a = jnp.exp(m_o - m)
            f = jnp.where(live, a / (l_o * a + l_p * jnp.exp(m_p - m)), 0.0)
            par = lane_pick(PARITY, o)
            fac[o, 0:heads, :] = f * (1.0 - par)
            fac[o, heads : 2 * heads, :] = f * par
            return carry

        lax.fori_loop(0, OWN, one, 0)

    def both(o, h, t0, t1):
        return jnp.concatenate([t0.astype(BF16), t1.astype(BF16)], axis=0)

    def value_one(o):
        gather_blocks(do_all, do_own, o)
        for h in range(heads):
            e = ex[o, h]
            p = both(o, h, e * fac[o, h : h + 1, :], e * fac[o, heads + h : heads + h + 1, :])
            t = lax.dot_general(p, do_own[o, :, cols(h)], NN, preferred_element_type=F32)
            dkv[1, o, :, cols(h)] = t.astype(BF16)

    def dots_one(o):
        par = lane_pick(PARITY, o)
        for h in range(heads):
            g = lax.dot_general(kv[1, o, :, cols(h)], do_own[o, :, cols(h)], NT, preferred_element_type=F32)
            g = jnp.where(par > 0.5, g[128:], g[:128])
            gw[o, h] = g
            f = fac[o, h : h + 1, :] + fac[o, heads + h : heads + h + 1, :]
            p = (ex[o, h] * f).astype(BF16).astype(F32)
            st2[y * OWN + o, h : h + 1, :] = jnp.sum(p * g, axis=0, keepdims=True)

    def key_one(o):
        _, live_p = lives(o)
        rd = st2[y * OWN + o][:heads] + jnp.where(live_p, partner_rows(st2, o, OTHER)[:heads], 0.0)
        for h in range(heads):
            e = ex[o, h]
            t = gw[o, h] - rd[h : h + 1]
            d = both(o, h, e * fac[o, h : h + 1, :] * t, e * fac[o, heads + h : heads + h + 1, :] * t)
            dk = lax.dot_general(d, q_own[o, :, cols(h)], NN, preferred_element_type=F32)
            dkv[0, o, :, cols(h)] = (dk * scale).astype(BF16)
            dq = lax.dot_general(d, kv[0, o, :, cols(h)], TN, preferred_element_type=F32)
            dqp[pl.ds(o * RDR, RDR), :, cols(h)] = (dq * scale).astype(BF16).reshape(RDR, BLOCK, HEAD)

    def per_owner(fn, dist):
        if dist in (0, 4):
            fn(zz(dist))
        else:

            def one(i, carry):
                fn(zz(dist * (1 - 2 * i)))
                return carry

            lax.fori_loop(0, 2, one, 0)

    def rs_buf(way, a, k, e):
        rows = pl.ds(e * 128, 128)
        if k == 3:
            return dkv_out.at[a, 1 if way == "R" else 2, rows]
        return (rsr if way == "R" else rsl).at[a, k, rows]

    def rs_hop(way, a, k, e):
        far = 0 if way == "R" else 1
        sign = 1 if way == "R" else -1
        o = zz(sign * (4 - k))
        piece = dkv.at[a, o, pl.ds(e * 128, 128)]
        if k > 1 or (k == 1 and e == far):
            rs_take(way, a, k - 1, e, o)
        send(("rs" + way, a, k, e), piece, rs_buf(way, a, k, e), at_z(sign))

    def rs_take(way, a, k, e, o):
        buf = rsr if way == "R" else rsl
        recv(("rs" + way, a, k, e), rs_buf(way, a, k, e))
        rows = pl.ds(e * 128, 128)
        dkv[a, o, rows, :] = (dkv[a, o, rows, :].astype(F32) + buf[a, k, rows, :].astype(F32)).astype(BF16)

    def rs_far(a, k):
        rs_hop("R", a, k, 0)
        rs_hop("L", a, k, 1)

    def rs_near(a, k):
        rs_hop("R", a, k, 1)
        rs_hop("L", a, k, 0)

    x_start()
    kv_first()
    for h in range(2):
        for way, part in (("R", HALVES[h]), ("L", HALVES[1 - h])):
            y_first("q", q_in.at[pl.ds(part[1], part[2])], q_all, part, way)
    send(("ogc", 0), og_in, og.at[mp], sibling)
    y_direct("cnt", None, cnt_all, 8)
    lax.fori_loop(0, RDR, tables, 0)

    x_on(0)
    for part in HALVES:
        y_on("q", q_all, part)
    kv_hop(1, 0)
    x_near(0)
    for cp in local:
        cp.wait()
    x_on(1)
    mm_own()
    kv_hop(1, 1)
    x_far(0)
    for d in (-1, 1, 2):
        mm(d, 0)
    grad_done(0)
    x_near(1)
    for part in HALVES:
        y_rest("q", q_all, part)
    y_direct_wait("cnt", cnt_all, 8)
    x_on(2)
    kv_hop(2, 0)
    scores(0)
    for d in (-1, 1):
        mm(d, 1)
    x_far(1)
    mm(2, 1)
    grad_done(1)
    do_on(0)
    x_near(2)
    kv_hop(2, 1)
    x_on(3)
    for d in (-1, 1):
        mm(d, 2)
    scores(1)
    x_far(2)
    mm(2, 2)
    grad_done(2)
    do_on(1)
    kv_hop(3, 0)
    x_near(3)
    x_on(4)
    for d in (-1, 1):
        mm(d, 3)
    x_far(3)
    mm(2, 3)
    grad_done(3)
    x_near(4)
    do_on(2)
    for d in (-1, 1):
        mm(d, 4)
    x_far(4)
    kv_hop(3, 1)
    mm(2, 4)
    grad_done(4)
    scores(2)
    do_on(3)
    scores(3)
    kv_hop(4, 0)
    scores(4)
    y_direct("st1", None, st1, OWN)
    do_on(4)
    kv_hop(4, 1)
    for g in range(4):
        y_rest("do", do_all, GROUPS[g])
    y_direct_wait("st1", st1, OWN)
    factors()
    y_rest("do", do_all, GROUPS[4])

    per_owner(value_one, 4)
    rs_far(1, 0)
    per_owner(value_one, 3)
    rs_near(1, 1)
    per_owner(value_one, 2)
    per_owner(dots_one, 4)
    rs_far(1, 1)
    for d in (1, 0):
        per_owner(value_one, d)
    rs_near(1, 2)
    for d in (3, 2):
        per_owner(dots_one, d)
    rs_far(1, 2)
    for d in (1, 0):
        per_owner(dots_one, d)
    y_direct("st2", None, st2, OWN)
    rs_near(1, 3)
    y_direct_wait("st2", st2, OWN)

    per_owner(key_one, 4)
    rs_far(0, 0)
    per_owner(key_one, 3)
    rs_near(0, 1)
    rs_far(1, 3)
    per_owner(key_one, 2)
    rs_far(0, 1)
    per_owner(key_one, 1)
    rs_near(0, 2)
    per_owner(key_one, 0)
    for a in range(2):
        local_copy(dkv.at[a, z], dkv_out.at[a, 0])

    def blocks(r, carry):
        def one(b, carry2):
            j = r * 16 + b * 2
            t = dqp[scal[PAIR + j]].astype(F32) * scal[MINE + j].astype(F32)
            t += dqp[scal[PAIR + 1 + j]].astype(F32) * scal[MINE + 1 + j].astype(F32)
            dqb[r * 8 + b] = t.astype(BF16)
            return carry2

        return lax.fori_loop(0, 8, one, carry)

    lax.fori_loop(0, RDR, blocks, 0)

    def dq_rows(d, h):
        return dqb.at[y_rows(d, HALVES[h])]

    def dq_land(way, h):
        return dq_out.at[1 if way == "R" else 2, pl.ds(h * 4, 4)]

    send(("dq", "R", "far"), dq_rows(2, 0), dq_far.at[pl.ds(0, 4)], at_y(1))
    send(("dq", "L", "far"), dq_rows(2, 1), dq_far.at[pl.ds(4, 4)], at_y(-1))
    send(("dq", "R", 1), dq_rows(1, 1), dq_land("R", 1), at_y(1))
    send(("dq", "L", 0), dq_rows(-1, 0), dq_land("L", 0), at_y(-1))
    local_copy(dqb.at[pl.ds(y * 8, 8)], dq_out.at[0])

    def dq_on(way, h, d):
        far = pl.ds(h * 4, 4)
        recv(("dq", way, "far"), dq_far.at[far])
        rows = y_rows(d, HALVES[h])
        dqb[rows] = (dqb[rows].astype(F32) + dq_far[far].astype(F32)).astype(BF16)
        send(("dq", way, h), dqb.at[rows], dq_land(way, h), at_y(d))

    rs_far(0, 2)
    rs_near(0, 3)
    dq_on("R", 0, 1)
    dq_on("L", 1, -1)
    rs_far(0, 3)

    def rs_last(a):
        for e in range(2):
            for way in ("R", "L"):
                recv(("rs" + way, a, 3, e), rs_buf(way, a, 3, e))

    for cp in local[LOCAL_IN:]:
        cp.wait()
    rs_last(1)
    for h in range(2):
        for way in ("R", "L"):
            recv(("dq", way, h), dq_land(way, h))
    rs_last(0)
    for cp in started:
        cp.wait_send()


def sums(dq_in, dkv_in, dq_out, dk_out, dv_out):
    def three(t):
        return (t[0].astype(F32) + t[1].astype(F32) + t[2].astype(F32)).astype(BF16)

    for b in range(8):
        dq_out[pl.ds(b * BLOCK, BLOCK), :] = three(dq_in[:, b])
    for out, a in ((dk_out, 0), (dv_out, 1)):
        for e in range(2):
            out[e] = three(dkv_in[a, :, pl.ds(e * 128, 128), :])


def on_device(out_grad, out_weight, queries, keys, values, retrieval, counts):
    tok, width = queries.shape
    heads = width // HEAD
    blocks = tok // BLOCK
    lanes = NY * BLOCK
    vm = pltpu.VMEM
    scratch = [
        vm((2 * NX, tok, 1024), BF16),
        vm((2 * NX, width, 1024), BF16),
        vm((tok, width), F32),
        vm((2, OWN, 256, width), BF16),
        vm((RDR * blocks, BLOCK, width), BF16),
        vm((RDR * blocks, BLOCK, width), BF16),
        vm((RDR * blocks, 8, lanes), F32),
        vm((OWN, lanes, width), BF16),
        vm((OWN, lanes, width), BF16),
        vm((OWN, heads, 128, lanes), F32),
        vm((OWN, heads, 128, lanes), F32),
        vm((NY * OWN, 8, lanes), F32),
        vm((NY * OWN, 8, lanes), F32),
        vm((OWN, 8, lanes), F32),
        vm((OWN * RDR, BLOCK, width), BF16),
        vm((2, OWN, 256, width), BF16),
        vm((2, 3, 256, width), BF16),
        vm((2, 3, 256, width), BF16),
        vm((RDR * blocks, BLOCK, width), BF16),
        vm((8, BLOCK, width), BF16),
        pltpu.SMEM((288,), jnp.int32),
        pltpu.SemaphoreType.DMA((MAX_COPIES,)),
        pltpu.SemaphoreType.DMA((MAX_COPIES,)),
        pltpu.SemaphoreType.DMA((16,)),
    ]
    hbm = pl.BlockSpec(memory_space=pl.ANY)
    vmem = pl.BlockSpec(memory_space=pltpu.VMEM)
    smem = pl.BlockSpec(memory_space=pltpu.SMEM)
    dq_parts, dkv_parts = pl.pallas_call(
        functools.partial(body, heads),
        out_shape=(
            jax.ShapeDtypeStruct((3, blocks, BLOCK, width), BF16),
            jax.ShapeDtypeStruct((2, 3, 256, width), BF16),
        ),
        in_specs=[smem, smem, hbm, hbm, hbm, hbm, hbm],
        out_specs=(hbm, hbm),
        scratch_shapes=scratch,
        compiler_params=pltpu.CompilerParams(
            collective_id=0, has_side_effects=True, vmem_limit_bytes=63 * 1024 * 1024
        ),
        name="column_attention_grad",
    )(
        retrieval.T,
        counts,
        out_grad,
        out_weight,
        queries.reshape(blocks, BLOCK, width),
        keys.reshape(256, width),
        values.reshape(256, width),
    )
    return pl.pallas_call(
        sums,
        out_shape=(
            jax.ShapeDtypeStruct(queries.shape, BF16),
            jax.ShapeDtypeStruct(keys.shape, BF16),
            jax.ShapeDtypeStruct(values.shape, BF16),
        ),
        in_specs=[vmem, vmem],
        out_specs=(vmem, vmem, vmem),
        name="sums_of_sides",
    )(dq_parts, dkv_parts)


def solution(mesh):
    return jax.shard_map(
        on_device,
        mesh=mesh,
        in_specs=(
            P("seq", "mp"),
            P("mp", None),
            P("seq", "mp"),
            P("seq", None, "mp"),
            P("seq", None, "mp"),
            P(),
            P("seq"),
        ),
        out_specs=(P("seq", "mp"), P("seq", None, "mp"), P("seq", None, "mp")),
        check_vma=False,
    )
```

```python
import functools
import math

import jax
import jax.numpy as jnp
from jax import lax
from jax.experimental import pallas as pl
from jax.experimental.pallas import tpu as pltpu
from jax.sharding import PartitionSpec as P

HEAD = 128
BLOCK = 64
NEIGH = 2
NX, NY, NZ = 4, 4, 8
OWN = NZ
RDR = NY
LOW = -1e30
MESH = pl.DeviceIdType.MESH
F32, BF16 = jnp.float32, jnp.bfloat16
NT = (((1,), (1,)), ((), ()))
NN = (((1,), (0,)), ((), ()))
TN = (((0,), (0,)), ((), ()))


class Ids:
    def __init__(self):
        self.at = {}

    def __call__(self, *name):
        return self.at.setdefault(name, len(self.at))


MAX_COPIES = 144
GROUPS = ((0, 0, 2), (1, 2, 2), (2, 4, 2), (3, 6, 1), (4, 7, 1))
HALVES = ((0, 0, 4), (1, 4, 4))
LOCAL_IN = 12
BLK, OTHER, PAIR, MINE, EXISTS, PLACE, PARITY = 0, 32, 64, 128, 192, 224, 256


def body(
    heads,
    ret,
    cnt_in,
    og_in,
    w_in,
    q_in,
    k_in,
    v_in,
    dq_out,
    dk_out,
    dv_out,
    og,
    w,
    acc,
    kv,
    q_all,
    do_all,
    cnt_all,
    q_own,
    do_own,
    ex,
    gw,
    st1,
    st2,
    fac,
    dqp,
    dkv,
    rsr,
    rsl,
    dqb,
    dq_far,
    dq_r,
    dq_l,
    scal,
    ssem,
    rsem,
    lsem,
):
    ids = Ids()
    scale = 1.0 / math.sqrt(HEAD)
    seq, mp = lax.axis_index("seq"), lax.axis_index("mp")
    y, z = seq // NZ, seq % NZ
    x, core = mp // 2, mp % 2

    def at_x(d):
        return (seq, ((x + d) % NX) * 2 + core)

    sibling = (seq, x * 2 + (1 - core))

    def at_y(d):
        return (((y + d) % NY) * NZ + z, mp)

    def at_z(d):
        return (y * NZ + (z + d) % NZ, mp)

    def zz(d):
        return (z + d) % NZ

    started = []
    drained = [0]

    def drain(leave=0):
        for cp in started[drained[0] : len(started) - leave]:
            cp.wait_send()
        drained[0] = max(drained[0], len(started) - leave)

    def send(name, src, dst, dev):
        i = ids(*name)
        cp = pltpu.make_async_remote_copy(
            src_ref=src, dst_ref=dst, send_sem=ssem.at[i], recv_sem=rsem.at[i], device_id=dev, device_id_type=MESH
        )
        cp.start()
        started.append(cp)

    def recv(name, dst):
        i = ids(*name)
        pltpu.make_async_remote_copy(
            src_ref=dst, dst_ref=dst, send_sem=ssem.at[i], recv_sem=rsem.at[i], device_id=sibling, device_id_type=MESH
        ).wait_recv()

    barrier = pltpu.get_barrier_semaphore()
    peers = [at_x(1), at_x(-1), sibling, at_y(1), at_y(-1), at_y(2), at_z(1), at_z(-1)]
    for dev in peers:
        pl.semaphore_signal(barrier, inc=1, device_id=dev, device_id_type=MESH)

    local = []

    def local_copy(src, dst):
        cp = pltpu.make_async_copy(src, dst, lsem.at[len(local)])
        cp.start()
        local.append(cp)

    local_copy(og_in, og.at[mp])
    for c in range(2 * NX):
        local_copy(w_in.at[:, pl.ds(c * 1024, 1024)], w.at[c])
    local_copy(q_in, q_all.at[pl.ds(y * 8, 8)])
    local_copy(k_in, kv.at[0, z])
    local_copy(v_in, kv.at[1, z])

    def tables(r, carry):
        base = (r * NZ + z) * 8
        named = [ret[j % 2, base + j // 2] for j in range(16)]
        owner = [e >> 1 for e in named]
        code = []
        for j in range(16):
            own = owner[j] - y * OWN
            near = (own >= 0) & (own < OWN)
            scal[PAIR + r * 16 + j] = jnp.where(near, own, 0) * RDR + r
            scal[MINE + r * 16 + j] = jnp.where(near, 1, 0)
            code.append((owner[j ^ 1] << 5) + ((named[j] & 1) << 4) + ((j % 2) << 3) + j // 2 + 1024)
        for o in range(OWN):
            t = 0
            for j in range(16):
                t = t + jnp.where(owner[j] == y * OWN + o, code[j], 0)
            scal[BLK + o * RDR + r] = r * 8 + (t & 7)
            scal[PLACE + o * RDR + r] = (t >> 3) & 1
            scal[PARITY + o * RDR + r] = (t >> 4) & 1
            scal[OTHER + o * RDR + r] = (t >> 5) & 31
            scal[EXISTS + o * RDR + r] = t >> 10
        return carry

    for b in range(8):
        cnt_all[y * 8 + b] = jnp.full((8, RDR * BLOCK), cnt_in[b].astype(F32))

    pl.semaphore_wait(barrier, len(peers))

    def kv_piece(a, o, e):
        return kv.at[a, o, pl.ds(e * 128, 128)]

    pieces = [(a, e) for a in range(2) for e in range(2)]

    def kv_first():
        for a, e in pieces:
            src = (k_in, v_in)[a].at[pl.ds(e * 128, 128)]
            send(("kvR", 1, a, e), src, kv_piece(a, z, e), at_z(1))
            send(("kvL", 1, a, e), src, kv_piece(a, z, e), at_z(-1))

    def kv_hop(k, a):
        for e in range(2):
            if k < 4 or e == 0:
                o = zz(-k)
                recv(("kvR", k, a, e), kv_piece(a, o, e))
                if k < 3 or (k == 3 and e == 0):
                    send(("kvR", k + 1, a, e), kv_piece(a, o, e), kv_piece(a, o, e), at_z(1))
            if k < 4 or e == 1:
                o = zz(k)
                recv(("kvL", k, a, e), kv_piece(a, o, e))
                if k < 3 or (k == 3 and e == 1):
                    send(("kvL", k + 1, a, e), kv_piece(a, o, e), kv_piece(a, o, e), at_z(-1))

    def y_rows(d, part):
        return pl.ds(((y + d) % NY) * 8 + part[1], part[2])

    def y_first(tag, src, buf, part, way):
        send((tag, way, part[0]), src, buf.at[y_rows(0, part)], at_y(1 if way == "R" else -1))

    def y_on(tag, buf, part):
        even = part[0] % 2 == 0
        rows = buf.at[y_rows(-1 if even else 1, part)]
        recv((tag, "R" if even else "L", part[0]), rows)
        send((tag, "F", part[0]), rows, rows, at_y(1 if even else -1))

    def y_rest(tag, buf, part):
        even = part[0] % 2 == 0
        recv((tag, "L" if even else "R", part[0]), buf.at[y_rows(1 if even else -1, part)])
        recv((tag, "F", part[0]), buf.at[y_rows(2, part)])

    def y_direct(tag, src, buf, rows):
        mine = buf.at[pl.ds(y * rows, rows)]
        for d in (1, -1, 2):
            send((tag, d), src if src is not None else mine, mine, at_y(d))

    def y_direct_wait(tag, buf, rows):
        for d in (1, -1, 2):
            recv((tag, d), buf.at[pl.ds(((y - d) % NY) * rows, rows)])

    def og_piece(d, g, i=None, other=False):
        c = ((x + d) % NX) * 2 + ((1 - core) if other else core)
        return og.at[c, og_rows(g, i)]

    def og_rows(g, i=None):
        _, b0, n = GROUPS[g]
        if i is None:
            return pl.ds(b0 * BLOCK, n * BLOCK)
        return pl.ds(b0 * BLOCK + i * (n * BLOCK // 2), n * BLOCK // 2)

    def x_own(way, g, i):
        if g < len(GROUPS):
            send(("og", way, g, i), og_in.at[og_rows(g, i)], og_piece(0, g, i), at_x(1 if way == "R" else -1))

    def x_start():
        for n in range(3):
            x_own("R", n // 2, n % 2)
            x_own("L", n // 2, 1 - n % 2)

    def x_on(g):
        for way, i, d in (("R", 0, -1), ("L", 1, 1)):
            piece = og_piece(d, g, i)
            recv(("og", way, g, i), piece)
            send(("og", "F", g, i), piece, piece, at_x(-d))
            x_own(way, g + 1, 1 - i)
            x_own(way, g + 2, i)

    def x_near(g):
        for way, i, d in (("R", 1, -1), ("L", 0, 1)):
            recv(("og", way, g, i), og_piece(d, g, i))
            piece = og_piece(d, g)
            send(("ogc", d, g), piece, piece, sibling)

    def x_far(g):
        for i in range(2):
            recv(("og", "F", g, i), og_piece(2, g, i))
        piece = og_piece(2, g)
        send(("ogc", 2, g), piece, piece, sibling)

    def mm_own():
        for c in (mp, x * 2 + 1 - core):
            p = lax.dot_general(og[c], w[c], NT, preferred_element_type=F32)
            if c is mp:
                acc[...] = p
                recv(("ogc", 0), og.at[x * 2 + 1 - core])
            else:
                acc[...] += p

    def mm(d, g):
        rows = og_rows(g)
        for other in (False, True):
            c = ((x + d) % NX) * 2 + ((1 - core) if other else core)
            if other:
                recv(("ogc", d, g), og_piece(d, g, None, True))
            acc[rows, :] += lax.dot_general(og[c, rows, :], w[c], NT, preferred_element_type=F32)

    def grad_done(g):
        n = GROUPS[g][2]
        do_all[y_rows(0, GROUPS[g])] = acc[og_rows(g), :].astype(BF16).reshape(n, BLOCK, heads * HEAD)
        src = do_all.at[y_rows(0, GROUPS[g])]
        for way in ("R", "L"):
            y_first("do", src, do_all, GROUPS[g], way)

    def do_on(g):
        y_on("do", do_all, GROUPS[g])

    lane_reader = lax.broadcasted_iota(jnp.int32, (8, RDR * BLOCK), 1) // BLOCK

    def lane_pick(base, o):
        t = jnp.full((8, RDR * BLOCK), scal[base + o * RDR])
        for r in range(1, RDR):
            t = jnp.where(lane_reader == r, scal[base + o * RDR + r], t)
        return t.astype(F32)[0:1]

    def gather_blocks(src, dst, o):
        for r in range(RDR):
            dst[o, pl.ds(r * BLOCK, BLOCK), :] = src[scal[BLK + o * RDR + r]]

    def partner_rows(buf, o, base):
        t = buf[scal[base + o * RDR]]
        for r in range(1, RDR):
            t = jnp.where(lane_reader == r, buf[scal[base + o * RDR + r]], t)
        return t

    def cols(h):
        return pl.ds(h * HEAD, HEAD)

    def score_one(o):
        gather_blocks(q_all, q_own, o)
        par = lane_pick(PARITY, o)
        for h in range(heads):
            s = lax.dot_general(kv[0, o, :, cols(h)], q_own[o, :, cols(h)], NT, preferred_element_type=F32)
            s = jnp.where(par > 0.5, s[128:], s[:128]) * scale
            m = jnp.max(s, axis=0, keepdims=True)
            e = jnp.exp(s - m)
            ex[o, h] = e
            st1[y * OWN + o, h : h + 1, :] = m
            st1[y * OWN + o, heads + h : heads + h + 1, :] = jnp.sum(e, axis=0, keepdims=True)

    def scores(dist):
        if dist in (0, 4):
            score_one(zz(dist))
        else:

            def one(i, carry):
                score_one(zz(dist * (1 - 2 * i)))
                return carry

            lax.fori_loop(0, 2, one, 0)

    def lives(o):
        exists, place = lane_pick(EXISTS, o), lane_pick(PLACE, o)
        short = 2.0 - partner_rows(cnt_all, o, BLK)[0:1, :]
        return exists * (1.0 - place * short) > 0.5, exists * (1.0 - (1.0 - place) * short) > 0.5

    def factors():
        def one(o, carry):
            live, live_p = lives(o)
            own = st1[y * OWN + o]
            oth = partner_rows(st1, o, OTHER)
            m_o, l_o = own[:heads], own[heads : 2 * heads]
            m_p = jnp.where(live_p, oth[:heads], LOW)
            l_p = jnp.where(live_p, oth[heads : 2 * heads], 0.0)
            m = jnp.maximum(m_o, m_p)
            a = jnp.exp(m_o - m)
            f = jnp.where(live, a / (l_o * a + l_p * jnp.exp(m_p - m)), 0.0)
            par = lane_pick(PARITY, o)
            fac[o, 0:heads, :] = f * (1.0 - par)
            fac[o, heads : 2 * heads, :] = f * par
            return carry

        lax.fori_loop(0, OWN, one, 0)

    def both(o, h, t0, t1):
        return jnp.concatenate([t0.astype(BF16), t1.astype(BF16)], axis=0)

    def value_one(o):
        gather_blocks(do_all, do_own, o)
        for h in range(heads):
            e = ex[o, h]
            p = both(o, h, e * fac[o, h : h + 1, :], e * fac[o, heads + h : heads + h + 1, :])
            t = lax.dot_general(p, do_own[o, :, cols(h)], NN, preferred_element_type=F32)
            dkv[1, o, :, cols(h)] = t.astype(BF16)

    def dots_one(o):
        par = lane_pick(PARITY, o)
        for h in range(heads):
            g = lax.dot_general(kv[1, o, :, cols(h)], do_own[o, :, cols(h)], NT, preferred_element_type=F32)
            g = jnp.where(par > 0.5, g[128:], g[:128])
            gw[o, h] = g
            f = fac[o, h : h + 1, :] + fac[o, heads + h : heads + h + 1, :]
            p = (ex[o, h] * f).astype(BF16).astype(F32)
            st2[y * OWN + o, h : h + 1, :] = jnp.sum(p * g, axis=0, keepdims=True)

    def key_one(o):
        _, live_p = lives(o)
        rd = st2[y * OWN + o][:heads] + jnp.where(live_p, partner_rows(st2, o, OTHER)[:heads], 0.0)
        for h in range(heads):
            e = ex[o, h]
            t = gw[o, h] - rd[h : h + 1]
            d = both(o, h, e * fac[o, h : h + 1, :] * t, e * fac[o, heads + h : heads + h + 1, :] * t)
            dk = lax.dot_general(d, q_own[o, :, cols(h)], NN, preferred_element_type=F32)
            dkv[0, o, :, cols(h)] = (dk * scale).astype(BF16)
            dq = lax.dot_general(d, kv[0, o, :, cols(h)], TN, preferred_element_type=F32)
            dqp[pl.ds(o * RDR, RDR), :, cols(h)] = (dq * scale).astype(BF16).reshape(RDR, BLOCK, HEAD)

    def per_owner(fn, dist):
        if dist in (0, 4):
            fn(zz(dist))
        else:

            def one(i, carry):
                fn(zz(dist * (1 - 2 * i)))
                return carry

            lax.fori_loop(0, 2, one, 0)

    def rs_buf(way, a, k, e):
        rows = pl.ds(e * 128, 128)
        if k == 3 and a == 0:
            return dk_out.at[1 if way == "R" else 2, rows]
        return (rsr if way == "R" else rsl).at[a, k, rows]

    def rs_hop(way, a, k, e):
        far = 0 if way == "R" else 1
        sign = 1 if way == "R" else -1
        o = zz(sign * (4 - k))
        piece = dkv.at[a, o, pl.ds(e * 128, 128)]
        if k > 1 or (k == 1 and e == far):
            rs_take(way, a, k - 1, e, o)
        send(("rs" + way, a, k, e), piece, rs_buf(way, a, k, e), at_z(sign))

    def rs_take(way, a, k, e, o):
        buf = rsr if way == "R" else rsl
        recv(("rs" + way, a, k, e), rs_buf(way, a, k, e))
        rows = pl.ds(e * 128, 128)
        dkv[a, o, rows, :] = (dkv[a, o, rows, :].astype(F32) + buf[a, k, rows, :].astype(F32)).astype(BF16)

    def rs_far(a, k):
        rs_hop("R", a, k, 0)
        rs_hop("L", a, k, 1)

    def rs_near(a, k):
        rs_hop("R", a, k, 1)
        rs_hop("L", a, k, 0)

    x_start()
    kv_first()
    for h in range(2):
        for way, part in (("R", HALVES[h]), ("L", HALVES[1 - h])):
            y_first("q", q_in.at[pl.ds(part[1], part[2])], q_all, part, way)
    send(("ogc", 0), og_in, og.at[mp], sibling)
    y_direct("cnt", None, cnt_all, 8)
    lax.fori_loop(0, RDR, tables, 0)

    x_on(0)
    for part in HALVES:
        y_on("q", q_all, part)
    kv_hop(1, 0)
    x_near(0)
    for cp in local:
        cp.wait()
    x_on(1)
    mm_own()
    kv_hop(1, 1)
    x_far(0)
    for d in (-1, 1, 2):
        mm(d, 0)
    grad_done(0)
    x_near(1)
    for part in HALVES:
        y_rest("q", q_all, part)
    y_direct_wait("cnt", cnt_all, 8)
    x_on(2)
    kv_hop(2, 0)
    scores(0)
    for d in (-1, 1):
        mm(d, 1)
    x_far(1)
    mm(2, 1)
    grad_done(1)
    do_on(0)
    x_near(2)
    kv_hop(2, 1)
    x_on(3)
    for d in (-1, 1):
        mm(d, 2)
    scores(1)
    x_far(2)
    mm(2, 2)
    grad_done(2)
    do_on(1)
    kv_hop(3, 0)
    x_near(3)
    x_on(4)
    for d in (-1, 1):
        mm(d, 3)
    x_far(3)
    mm(2, 3)
    grad_done(3)
    x_near(4)
    do_on(2)
    for d in (-1, 1):
        mm(d, 4)
    x_far(4)
    kv_hop(3, 1)
    mm(2, 4)
    grad_done(4)
    scores(2)
    do_on(3)
    scores(3)
    kv_hop(4, 0)
    scores(4)
    y_direct("st1", None, st1, OWN)
    do_on(4)
    kv_hop(4, 1)
    for g in range(4):
        y_rest("do", do_all, GROUPS[g])
    y_direct_wait("st1", st1, OWN)
    factors()
    y_rest("do", do_all, GROUPS[4])

    per_owner(value_one, 4)
    rs_far(1, 0)
    per_owner(value_one, 3)
    rs_near(1, 1)
    per_owner(value_one, 2)
    per_owner(dots_one, 4)
    rs_far(1, 1)
    for d in (1, 0):
        per_owner(value_one, d)
    rs_near(1, 2)
    for d in (3, 2):
        per_owner(dots_one, d)
    rs_far(1, 2)
    for d in (1, 0):
        per_owner(dots_one, d)
    y_direct("st2", None, st2, OWN)
    drain(14)
    y_direct_wait("st2", st2, OWN)

    per_owner(key_one, 4)
    rs_far(0, 0)
    per_owner(key_one, 3)
    rs_near(0, 1)
    rs_near(1, 3)
    per_owner(key_one, 2)
    rs_far(0, 1)
    per_owner(key_one, 1)
    rs_near(0, 2)
    rs_far(1, 3)
    per_owner(key_one, 0)
    local_copy(dkv.at[0, z], dk_out.at[0])

    def blocks(r, carry):
        def one(b, carry2):
            j = r * 16 + b * 2
            t = dqp[scal[PAIR + j]].astype(F32) * scal[MINE + j].astype(F32)
            t += dqp[scal[PAIR + 1 + j]].astype(F32) * scal[MINE + 1 + j].astype(F32)
            dqb[r * 8 + b] = t.astype(BF16)
            return carry2

        return lax.fori_loop(0, 8, one, carry)

    lax.fori_loop(0, RDR, blocks, 0)

    def dq_rows(d, h):
        return dqb.at[y_rows(d, HALVES[h])]

    def dq_land(way, h):
        return (dq_r if way == "R" else dq_l).at[pl.ds(h * 4, 4)]

    send(("dq", "R", "far"), dq_rows(2, 0), dq_far.at[pl.ds(0, 4)], at_y(1))
    send(("dq", "L", "far"), dq_rows(2, 1), dq_far.at[pl.ds(4, 4)], at_y(-1))
    send(("dq", "R", 1), dq_rows(1, 1), dq_land("R", 1), at_y(1))
    send(("dq", "L", 0), dq_rows(-1, 0), dq_land("L", 0), at_y(-1))

    def dq_on(way, h, d):
        far = pl.ds(h * 4, 4)
        recv(("dq", way, "far"), dq_far.at[far])
        rows = y_rows(d, HALVES[h])
        dqb[rows] = (dqb[rows].astype(F32) + dq_far[far].astype(F32)).astype(BF16)
        send(("dq", way, h), dqb.at[rows], dq_land(way, h), at_y(d))

    rs_far(0, 2)
    rs_near(0, 3)
    dq_on("R", 0, 1)
    dq_on("L", 1, -1)
    rs_far(0, 3)

    def rs_last(a):
        for e in range(2):
            for way in ("R", "L"):
                recv(("rs" + way, a, 3, e), rs_buf(way, a, 3, e))

    def three(a, b, c):
        return (a.astype(F32) + b.astype(F32) + c.astype(F32)).astype(BF16)

    rs_last(1)
    dkv[1, z] = three(dkv[1, z], rsr[1, 3], rsl[1, 3])
    local_copy(dkv.at[1, z], dv_out)
    for h in range(2):
        for way in ("R", "L"):
            recv(("dq", way, h), dq_land(way, h))
    own = pl.ds(y * 8, 8)
    dqb[own] = three(dqb[own], dq_r[...], dq_l[...])
    local_copy(dqb.at[own], dq_out)
    drain(4)
    for cp in local[LOCAL_IN:]:
        cp.wait()
    rs_last(0)
    drain()


def finish(dq_in, dk_in, dv_in, dq_out, dk_out, dv_out, dq, dk, dv, total, sem):
    takes = [
        pltpu.make_async_copy(src, dst, sem.at[i])
        for i, (src, dst) in enumerate(((dk_in, dk), (dv_in, dv), (dq_in, dq)))
    ]
    gives = [
        pltpu.make_async_copy(src, dst, sem.at[3 + i])
        for i, (src, dst) in enumerate(((total, dk_out), (dv, dv_out), (dq, dq_out)))
    ]
    for take in takes:
        take.start()
    takes[0].wait()
    total[...] = (dk[0].astype(F32) + dk[1].astype(F32) + dk[2].astype(F32)).astype(BF16)
    gives[0].start()
    for i in (1, 2):
        takes[i].wait()
        gives[i].start()
    for give in gives:
        give.wait()


def on_device(out_grad, out_weight, queries, keys, values, retrieval, counts):
    tok, width = queries.shape
    heads = width // HEAD
    blocks = tok // BLOCK
    lanes = NY * BLOCK
    vm = pltpu.VMEM
    scratch = [
        vm((2 * NX, tok, 1024), BF16),
        vm((2 * NX, width, 1024), BF16),
        vm((tok, width), F32),
        vm((2, OWN, 256, width), BF16),
        vm((RDR * blocks, BLOCK, width), BF16),
        vm((RDR * blocks, BLOCK, width), BF16),
        vm((RDR * blocks, 8, lanes), F32),
        vm((OWN, lanes, width), BF16),
        vm((OWN, lanes, width), BF16),
        vm((OWN, heads, 128, lanes), F32),
        vm((OWN, heads, 128, lanes), F32),
        vm((NY * OWN, 8, lanes), F32),
        vm((NY * OWN, 8, lanes), F32),
        vm((OWN, 8, lanes), F32),
        vm((OWN * RDR, BLOCK, width), BF16),
        vm((2, OWN, 256, width), BF16),
        vm((2, 4, 256, width), BF16),
        vm((2, 4, 256, width), BF16),
        vm((RDR * blocks, BLOCK, width), BF16),
        vm((8, BLOCK, width), BF16),
        vm((8, BLOCK, width), BF16),
        vm((8, BLOCK, width), BF16),
        pltpu.SMEM((288,), jnp.int32),
        pltpu.SemaphoreType.DMA((MAX_COPIES,)),
        pltpu.SemaphoreType.DMA((MAX_COPIES,)),
        pltpu.SemaphoreType.DMA((16,)),
    ]
    hbm = pl.BlockSpec(memory_space=pl.ANY)
    smem = pl.BlockSpec(memory_space=pltpu.SMEM)
    dq, dk_parts, dv = pl.pallas_call(
        functools.partial(body, heads),
        out_shape=(
            jax.ShapeDtypeStruct((blocks, BLOCK, width), BF16),
            jax.ShapeDtypeStruct((3, 256, width), BF16),
            jax.ShapeDtypeStruct((256, width), BF16),
        ),
        in_specs=[smem, smem, hbm, hbm, hbm, hbm, hbm],
        out_specs=(hbm, hbm, hbm),
        scratch_shapes=scratch,
        compiler_params=pltpu.CompilerParams(
            collective_id=0, has_side_effects=True, vmem_limit_bytes=63 * 1024 * 1024
        ),
        name="column_attention_grad",
    )(
        retrieval.T,
        counts,
        out_grad,
        out_weight,
        queries.reshape(blocks, BLOCK, width),
        keys.reshape(256, width),
        values.reshape(256, width),
    )
    dq, dk, dv = pl.pallas_call(
        finish,
        out_shape=(
            jax.ShapeDtypeStruct((blocks, BLOCK, width), BF16),
            jax.ShapeDtypeStruct((256, width), BF16),
            jax.ShapeDtypeStruct((256, width), BF16),
        ),
        in_specs=[hbm, hbm, hbm],
        out_specs=(hbm, hbm, hbm),
        scratch_shapes=[
            vm((blocks, BLOCK, width), BF16),
            vm((3, 256, width), BF16),
            vm((256, width), BF16),
            vm((256, width), BF16),
            pltpu.SemaphoreType.DMA((6,)),
        ],
        name="finish_outputs",
    )(dq, dk_parts, dv)
    return dq.reshape(queries.shape), dk.reshape(keys.shape), dv.reshape(values.shape)


def solution(mesh):
    return jax.shard_map(
        on_device,
        mesh=mesh,
        in_specs=(
            P("seq", "mp"),
            P("mp", None),
            P("seq", "mp"),
            P("seq", None, "mp"),
            P("seq", None, "mp"),
            P(),
            P("seq"),
        ),
        out_specs=(P("seq", "mp"), P("seq", None, "mp"), P("seq", None, "mp")),
        check_vma=False,
    )
```

```python
import functools
import math

import jax
import jax.numpy as jnp
from jax import lax
from jax.experimental import pallas as pl
from jax.experimental.pallas import tpu as pltpu
from jax.sharding import PartitionSpec as P

HEAD = 128
BLOCK = 64
NEIGH = 2
NX, NY, NZ = 4, 4, 8
OWN = NZ
RDR = NY
LOW = -1e30
MESH = pl.DeviceIdType.MESH
F32, BF16 = jnp.float32, jnp.bfloat16
NT = (((1,), (1,)), ((), ()))
NN = (((1,), (0,)), ((), ()))
TN = (((0,), (0,)), ((), ()))


class Ids:
    def __init__(self):
        self.at = {}

    def __call__(self, *name):
        return self.at.setdefault(name, len(self.at))


MAX_COPIES = 144
GROUPS = ((0, 0, 2), (1, 2, 2), (2, 4, 2), (3, 6, 1), (4, 7, 1))
HALVES = ((0, 0, 4), (1, 4, 4))
LOCAL_IN = 14
BLK, OTHER, PAIR, MINE, EXISTS, PLACE, PARITY = 0, 32, 64, 128, 192, 224, 256


def body(
    heads,
    ret_in,
    cnt_hbm,
    og_in,
    w_in,
    q_in,
    k_in,
    v_in,
    dq_out,
    dk_out,
    dv_out,
    og,
    w,
    acc,
    kv,
    q_all,
    do_all,
    cnt_all,
    q_own,
    do_own,
    ex,
    gw,
    st1,
    st2,
    fac,
    dqp,
    dkv,
    rsr,
    rsl,
    dqb,
    dq_far,
    dq_r,
    dq_l,
    ret,
    cnt_in,
    scal,
    ssem,
    rsem,
    lsem,
):
    ids = Ids()
    scale = 1.0 / math.sqrt(HEAD)
    seq, mp = lax.axis_index("seq"), lax.axis_index("mp")
    y, z = seq // NZ, seq % NZ
    x, core = mp // 2, mp % 2

    def at_x(d):
        return (seq, ((x + d) % NX) * 2 + core)

    sibling = (seq, x * 2 + (1 - core))

    def at_y(d):
        return (((y + d) % NY) * NZ + z, mp)

    def at_z(d):
        return (y * NZ + (z + d) % NZ, mp)

    def zz(d):
        return (z + d) % NZ

    started = []
    drained = [0]

    def drain(leave=0):
        for cp in started[drained[0] : len(started) - leave]:
            cp.wait_send()
        drained[0] = max(drained[0], len(started) - leave)

    def send(name, src, dst, dev):
        i = ids(*name)
        cp = pltpu.make_async_remote_copy(
            src_ref=src, dst_ref=dst, send_sem=ssem.at[i], recv_sem=rsem.at[i], device_id=dev, device_id_type=MESH
        )
        cp.start()
        started.append(cp)

    def recv(name, dst):
        i = ids(*name)
        pltpu.make_async_remote_copy(
            src_ref=dst, dst_ref=dst, send_sem=ssem.at[i], recv_sem=rsem.at[i], device_id=sibling, device_id_type=MESH
        ).wait_recv()

    barrier = pltpu.get_barrier_semaphore()
    peers = [at_x(1), at_x(-1), sibling, at_y(1), at_y(-1), at_y(2), at_z(1), at_z(-1)]
    for dev in peers:
        pl.semaphore_signal(barrier, inc=1, device_id=dev, device_id_type=MESH)

    local = []

    def local_copy(src, dst):
        cp = pltpu.make_async_copy(src, dst, lsem.at[len(local)])
        cp.start()
        local.append(cp)

    local_copy(ret_in, ret)
    local_copy(cnt_hbm, cnt_in)
    local_copy(og_in, og.at[mp])
    for c in range(2 * NX):
        local_copy(w_in.at[:, pl.ds(c * 1024, 1024)], w.at[c])
    local_copy(q_in, q_all.at[pl.ds(y * 8, 8)])
    local_copy(k_in, kv.at[0, z])
    local_copy(v_in, kv.at[1, z])

    def tables(r, carry):
        base = (r * NZ + z) * 8
        named = [ret[j % 2, base + j // 2] for j in range(16)]
        owner = [e >> 1 for e in named]
        code = []
        for j in range(16):
            own = owner[j] - y * OWN
            near = (own >= 0) & (own < OWN)
            scal[PAIR + r * 16 + j] = jnp.where(near, own, 0) * RDR + r
            scal[MINE + r * 16 + j] = jnp.where(near, 1, 0)
            code.append((owner[j ^ 1] << 5) + ((named[j] & 1) << 4) + ((j % 2) << 3) + j // 2 + 1024)
        for o in range(OWN):
            t = 0
            for j in range(16):
                t = t + jnp.where(owner[j] == y * OWN + o, code[j], 0)
            scal[BLK + o * RDR + r] = r * 8 + (t & 7)
            scal[PLACE + o * RDR + r] = (t >> 3) & 1
            scal[PARITY + o * RDR + r] = (t >> 4) & 1
            scal[OTHER + o * RDR + r] = (t >> 5) & 31
            scal[EXISTS + o * RDR + r] = t >> 10
        return carry

    def count_rows():
        for b in range(8):
            cnt_all[y * 8 + b] = jnp.full((8, RDR * BLOCK), cnt_in[b].astype(F32))


    pl.semaphore_wait(barrier, len(peers))

    def kv_piece(a, o, e):
        return kv.at[a, o, pl.ds(e * 128, 128)]

    pieces = [(a, e) for a in range(2) for e in range(2)]

    def kv_first():
        for a, e in pieces:
            src = (k_in, v_in)[a].at[pl.ds(e * 128, 128)]
            send(("kvR", 1, a, e), src, kv_piece(a, z, e), at_z(1))
            send(("kvL", 1, a, e), src, kv_piece(a, z, e), at_z(-1))

    def kv_hop(k, a):
        for e in range(2):
            if k < 4 or e == 0:
                o = zz(-k)
                recv(("kvR", k, a, e), kv_piece(a, o, e))
                if k < 3 or (k == 3 and e == 0):
                    send(("kvR", k + 1, a, e), kv_piece(a, o, e), kv_piece(a, o, e), at_z(1))
            if k < 4 or e == 1:
                o = zz(k)
                recv(("kvL", k, a, e), kv_piece(a, o, e))
                if k < 3 or (k == 3 and e == 1):
                    send(("kvL", k + 1, a, e), kv_piece(a, o, e), kv_piece(a, o, e), at_z(-1))

    def y_rows(d, part):
        return pl.ds(((y + d) % NY) * 8 + part[1], part[2])

    def y_first(tag, src, buf, part, way):
        send((tag, way, part[0]), src, buf.at[y_rows(0, part)], at_y(1 if way == "R" else -1))

    def y_on(tag, buf, part):
        even = part[0] % 2 == 0
        rows = buf.at[y_rows(-1 if even else 1, part)]
        recv((tag, "R" if even else "L", part[0]), rows)
        send((tag, "F", part[0]), rows, rows, at_y(1 if even else -1))

    def y_rest(tag, buf, part):
        even = part[0] % 2 == 0
        recv((tag, "L" if even else "R", part[0]), buf.at[y_rows(1 if even else -1, part)])
        recv((tag, "F", part[0]), buf.at[y_rows(2, part)])

    def y_direct(tag, src, buf, rows):
        mine = buf.at[pl.ds(y * rows, rows)]
        for d in (1, -1, 2):
            send((tag, d), src if src is not None else mine, mine, at_y(d))

    def y_direct_wait(tag, buf, rows):
        for d in (1, -1, 2):
            recv((tag, d), buf.at[pl.ds(((y - d) % NY) * rows, rows)])

    def og_piece(d, g, i=None, other=False):
        c = ((x + d) % NX) * 2 + ((1 - core) if other else core)
        return og.at[c, og_rows(g, i)]

    def og_rows(g, i=None):
        _, b0, n = GROUPS[g]
        if i is None:
            return pl.ds(b0 * BLOCK, n * BLOCK)
        return pl.ds(b0 * BLOCK + i * (n * BLOCK // 2), n * BLOCK // 2)

    def x_own(way, g, i):
        if g < len(GROUPS):
            send(("og", way, g, i), og_in.at[og_rows(g, i)], og_piece(0, g, i), at_x(1 if way == "R" else -1))

    def x_start():
        for n in range(3):
            x_own("R", n // 2, n % 2)
            x_own("L", n // 2, 1 - n % 2)

    def x_on(g):
        for way, i, d in (("R", 0, -1), ("L", 1, 1)):
            piece = og_piece(d, g, i)
            recv(("og", way, g, i), piece)
            send(("og", "F", g, i), piece, piece, at_x(-d))
            x_own(way, g + 1, 1 - i)
            x_own(way, g + 2, i)

    def x_near(g):
        for way, i, d in (("R", 1, -1), ("L", 0, 1)):
            recv(("og", way, g, i), og_piece(d, g, i))
            piece = og_piece(d, g)
            send(("ogc", d, g), piece, piece, sibling)

    def x_far(g):
        for i in range(2):
            recv(("og", "F", g, i), og_piece(2, g, i))
        piece = og_piece(2, g)
        send(("ogc", 2, g), piece, piece, sibling)

    def mm_own():
        for c in (mp, x * 2 + 1 - core):
            p = lax.dot_general(og[c], w[c], NT, preferred_element_type=F32)
            if c is mp:
                acc[...] = p
                recv(("ogc", 0), og.at[x * 2 + 1 - core])
            else:
                acc[...] += p

    def mm(d, g):
        rows = og_rows(g)
        for other in (False, True):
            c = ((x + d) % NX) * 2 + ((1 - core) if other else core)
            if other:
                recv(("ogc", d, g), og_piece(d, g, None, True))
            acc[rows, :] += lax.dot_general(og[c, rows, :], w[c], NT, preferred_element_type=F32)

    def grad_done(g):
        n = GROUPS[g][2]
        do_all[y_rows(0, GROUPS[g])] = acc[og_rows(g), :].astype(BF16).reshape(n, BLOCK, heads * HEAD)
        src = do_all.at[y_rows(0, GROUPS[g])]
        for way in ("R", "L"):
            y_first("do", src, do_all, GROUPS[g], way)

    def do_on(g):
        y_on("do", do_all, GROUPS[g])

    lane_reader = lax.broadcasted_iota(jnp.int32, (8, RDR * BLOCK), 1) // BLOCK

    def lane_pick(base, o):
        t = jnp.full((8, RDR * BLOCK), scal[base + o * RDR])
        for r in range(1, RDR):
            t = jnp.where(lane_reader == r, scal[base + o * RDR + r], t)
        return t.astype(F32)[0:1]

    def gather_blocks(src, dst, o):
        for r in range(RDR):
            dst[o, pl.ds(r * BLOCK, BLOCK), :] = src[scal[BLK + o * RDR + r]]

    def partner_rows(buf, o, base):
        t = buf[scal[base + o * RDR]]
        for r in range(1, RDR):
            t = jnp.where(lane_reader == r, buf[scal[base + o * RDR + r]], t)
        return t

    def cols(h):
        return pl.ds(h * HEAD, HEAD)

    def score_one(o):
        gather_blocks(q_all, q_own, o)
        par = lane_pick(PARITY, o)
        for h in range(heads):
            s = lax.dot_general(kv[0, o, :, cols(h)], q_own[o, :, cols(h)], NT, preferred_element_type=F32)
            s = jnp.where(par > 0.5, s[128:], s[:128]) * scale
            m = jnp.max(s, axis=0, keepdims=True)
            e = jnp.exp(s - m)
            ex[o, h] = e
            st1[y * OWN + o, h : h + 1, :] = m
            st1[y * OWN + o, heads + h : heads + h + 1, :] = jnp.sum(e, axis=0, keepdims=True)

    def scores(dist):
        if dist in (0, 4):
            score_one(zz(dist))
        else:

            def one(i, carry):
                score_one(zz(dist * (1 - 2 * i)))
                return carry

            lax.fori_loop(0, 2, one, 0)

    def lives(o):
        exists, place = lane_pick(EXISTS, o), lane_pick(PLACE, o)
        short = 2.0 - partner_rows(cnt_all, o, BLK)[0:1, :]
        return exists * (1.0 - place * short) > 0.5, exists * (1.0 - (1.0 - place) * short) > 0.5

    def factors():
        def one(o, carry):
            live, live_p = lives(o)
            own = st1[y * OWN + o]
            oth = partner_rows(st1, o, OTHER)
            m_o, l_o = own[:heads], own[heads : 2 * heads]
            m_p = jnp.where(live_p, oth[:heads], LOW)
            l_p = jnp.where(live_p, oth[heads : 2 * heads], 0.0)
            m = jnp.maximum(m_o, m_p)
            a = jnp.exp(m_o - m)
            f = jnp.where(live, a / (l_o * a + l_p * jnp.exp(m_p - m)), 0.0)
            par = lane_pick(PARITY, o)
            fac[o, 0:heads, :] = f * (1.0 - par)
            fac[o, heads : 2 * heads, :] = f * par
            return carry

        lax.fori_loop(0, OWN, one, 0)

    def both(o, h, t0, t1):
        return jnp.concatenate([t0.astype(BF16), t1.astype(BF16)], axis=0)

    def value_one(o):
        gather_blocks(do_all, do_own, o)
        for h in range(heads):
            e = ex[o, h]
            p = both(o, h, e * fac[o, h : h + 1, :], e * fac[o, heads + h : heads + h + 1, :])
            t = lax.dot_general(p, do_own[o, :, cols(h)], NN, preferred_element_type=F32)
            dkv[1, o, :, cols(h)] = t.astype(BF16)

    def dots_one(o):
        par = lane_pick(PARITY, o)
        for h in range(heads):
            g = lax.dot_general(kv[1, o, :, cols(h)], do_own[o, :, cols(h)], NT, preferred_element_type=F32)
            g = jnp.where(par > 0.5, g[128:], g[:128])
            gw[o, h] = g
            f = fac[o, h : h + 1, :] + fac[o, heads + h : heads + h + 1, :]
            p = (ex[o, h] * f).astype(BF16).astype(F32)
            st2[y * OWN + o, h : h + 1, :] = jnp.sum(p * g, axis=0, keepdims=True)

    def key_one(o):
        _, live_p = lives(o)
        rd = st2[y * OWN + o][:heads] + jnp.where(live_p, partner_rows(st2, o, OTHER)[:heads], 0.0)
        for h in range(heads):
            e = ex[o, h]
            t = gw[o, h] - rd[h : h + 1]
            d = both(o, h, e * fac[o, h : h + 1, :] * t, e * fac[o, heads + h : heads + h + 1, :] * t)
            dk = lax.dot_general(d, q_own[o, :, cols(h)], NN, preferred_element_type=F32)
            dkv[0, o, :, cols(h)] = (dk * scale).astype(BF16)
            dq = lax.dot_general(d, kv[0, o, :, cols(h)], TN, preferred_element_type=F32)
            dqp[pl.ds(o * RDR, RDR), :, cols(h)] = (dq * scale).astype(BF16).reshape(RDR, BLOCK, HEAD)

    def per_owner(fn, dist):
        if dist in (0, 4):
            fn(zz(dist))
        else:

            def one(i, carry):
                fn(zz(dist * (1 - 2 * i)))
                return carry

            lax.fori_loop(0, 2, one, 0)

    def rs_buf(way, a, k, e):
        rows = pl.ds(e * 128, 128)
        if k == 3 and a == 0:
            return dk_out.at[1 if way == "R" else 2, rows]
        return (rsr if way == "R" else rsl).at[a, k, rows]

    def rs_hop(way, a, k, e):
        far = 0 if way == "R" else 1
        sign = 1 if way == "R" else -1
        o = zz(sign * (4 - k))
        piece = dkv.at[a, o, pl.ds(e * 128, 128)]
        if k > 1 or (k == 1 and e == far):
            rs_take(way, a, k - 1, e, o)
        send(("rs" + way, a, k, e), piece, rs_buf(way, a, k, e), at_z(sign))

    def rs_take(way, a, k, e, o):
        buf = rsr if way == "R" else rsl
        recv(("rs" + way, a, k, e), rs_buf(way, a, k, e))
        rows = pl.ds(e * 128, 128)
        dkv[a, o, rows, :] = (dkv[a, o, rows, :].astype(F32) + buf[a, k, rows, :].astype(F32)).astype(BF16)

    def rs_far(a, k):
        rs_hop("R", a, k, 0)
        rs_hop("L", a, k, 1)

    def rs_near(a, k):
        rs_hop("R", a, k, 1)
        rs_hop("L", a, k, 0)

    x_start()
    kv_first()
    for h in range(2):
        for way, part in (("R", HALVES[h]), ("L", HALVES[1 - h])):
            y_first("q", q_in.at[pl.ds(part[1], part[2])], q_all, part, way)
    send(("ogc", 0), og_in, og.at[mp], sibling)
    for cp in local[:2]:
        cp.wait()
    count_rows()
    y_direct("cnt", None, cnt_all, 8)
    lax.fori_loop(0, RDR, tables, 0)

    x_on(0)
    for part in HALVES:
        y_on("q", q_all, part)
    kv_hop(1, 0)
    x_near(0)
    for cp in local[2:]:
        cp.wait()
    x_on(1)
    mm_own()
    kv_hop(1, 1)
    x_far(0)
    for d in (-1, 1, 2):
        mm(d, 0)
    grad_done(0)
    x_near(1)
    for part in HALVES:
        y_rest("q", q_all, part)
    y_direct_wait("cnt", cnt_all, 8)
    x_on(2)
    kv_hop(2, 0)
    scores(0)
    for d in (-1, 1):
        mm(d, 1)
    x_far(1)
    mm(2, 1)
    grad_done(1)
    do_on(0)
    x_near(2)
    kv_hop(2, 1)
    x_on(3)
    for d in (-1, 1):
        mm(d, 2)
    scores(1)
    x_far(2)
    mm(2, 2)
    grad_done(2)
    do_on(1)
    kv_hop(3, 0)
    x_near(3)
    x_on(4)
    for d in (-1, 1):
        mm(d, 3)
    x_far(3)
    mm(2, 3)
    grad_done(3)
    x_near(4)
    do_on(2)
    for d in (-1, 1):
        mm(d, 4)
    x_far(4)
    kv_hop(3, 1)
    mm(2, 4)
    grad_done(4)
    scores(2)
    do_on(3)
    scores(3)
    kv_hop(4, 0)
    scores(4)
    y_direct("st1", None, st1, OWN)
    do_on(4)
    kv_hop(4, 1)
    for g in range(4):
        y_rest("do", do_all, GROUPS[g])
    y_direct_wait("st1", st1, OWN)
    factors()
    y_rest("do", do_all, GROUPS[4])

    per_owner(value_one, 4)
    rs_far(1, 0)
    per_owner(value_one, 3)
    rs_near(1, 1)
    for d in (2, 1, 0):
        per_owner(value_one, d)
    for d in (4, 3, 2, 1, 0):
        per_owner(dots_one, d)
    y_direct("st2", None, st2, OWN)
    rs_far(1, 1)
    rs_near(1, 2)
    rs_far(1, 2)
    drain(14)
    y_direct_wait("st2", st2, OWN)

    per_owner(key_one, 4)
    rs_far(0, 0)
    per_owner(key_one, 3)
    rs_near(0, 1)
    rs_near(1, 3)
    per_owner(key_one, 2)
    rs_far(0, 1)
    per_owner(key_one, 1)
    rs_near(0, 2)
    rs_far(1, 3)
    per_owner(key_one, 0)
    local_copy(dkv.at[0, z], dk_out.at[0])

    def blocks(r, carry):
        def one(b, carry2):
            j = r * 16 + b * 2
            t = dqp[scal[PAIR + j]].astype(F32) * scal[MINE + j].astype(F32)
            t += dqp[scal[PAIR + 1 + j]].astype(F32) * scal[MINE + 1 + j].astype(F32)
            dqb[r * 8 + b] = t.astype(BF16)
            return carry2

        return lax.fori_loop(0, 8, one, carry)

    lax.fori_loop(0, RDR, blocks, 0)

    def dq_rows(d, h):
        return dqb.at[y_rows(d, HALVES[h])]

    def dq_land(way, h):
        return (dq_r if way == "R" else dq_l).at[pl.ds(h * 4, 4)]

    send(("dq", "R", "far"), dq_rows(2, 0), dq_far.at[pl.ds(0, 4)], at_y(1))
    send(("dq", "L", "far"), dq_rows(2, 1), dq_far.at[pl.ds(4, 4)], at_y(-1))
    send(("dq", "R", 1), dq_rows(1, 1), dq_land("R", 1), at_y(1))
    send(("dq", "L", 0), dq_rows(-1, 0), dq_land("L", 0), at_y(-1))

    def dq_on(way, h, d):
        far = pl.ds(h * 4, 4)
        recv(("dq", way, "far"), dq_far.at[far])
        rows = y_rows(d, HALVES[h])
        dqb[rows] = (dqb[rows].astype(F32) + dq_far[far].astype(F32)).astype(BF16)
        send(("dq", way, h), dqb.at[rows], dq_land(way, h), at_y(d))

    rs_far(0, 2)
    rs_near(0, 3)
    dq_on("R", 0, 1)
    dq_on("L", 1, -1)
    rs_far(0, 3)

    def rs_last(a):
        for e in range(2):
            for way in ("R", "L"):
                recv(("rs" + way, a, 3, e), rs_buf(way, a, 3, e))

    def three(a, b, c):
        return (a.astype(F32) + b.astype(F32) + c.astype(F32)).astype(BF16)

    rs_last(1)
    dkv[1, z] = three(dkv[1, z], rsr[1, 3], rsl[1, 3])
    local_copy(dkv.at[1, z], dv_out)
    for h in range(2):
        for way in ("R", "L"):
            recv(("dq", way, h), dq_land(way, h))
    own = pl.ds(y * 8, 8)
    dqb[own] = three(dqb[own], dq_r[...], dq_l[...])
    local_copy(dqb.at[own], dq_out)
    drain(4)
    for cp in local[LOCAL_IN:]:
        cp.wait()
    rs_last(0)
    drain()


def finish(dq_in, dk_in, dv_in, dq_out, dk_out, dv_out, dq, dk, dv, total, sem):
    takes = [
        pltpu.make_async_copy(src, dst, sem.at[i])
        for i, (src, dst) in enumerate(((dk_in, dk), (dv_in, dv), (dq_in, dq)))
    ]
    gives = [
        pltpu.make_async_copy(src, dst, sem.at[3 + i])
        for i, (src, dst) in enumerate(((total, dk_out), (dv, dv_out), (dq, dq_out)))
    ]
    for take in takes:
        take.start()
    takes[0].wait()
    total[...] = (dk[0].astype(F32) + dk[1].astype(F32) + dk[2].astype(F32)).astype(BF16)
    gives[0].start()
    for i in (1, 2):
        takes[i].wait()
        gives[i].start()
    for give in gives:
        give.wait()


def on_device(out_grad, out_weight, queries, keys, values, retrieval, counts):
    tok, width = queries.shape
    heads = width // HEAD
    blocks = tok // BLOCK
    lanes = NY * BLOCK
    vm = pltpu.VMEM
    scratch = [
        vm((2 * NX, tok, 1024), BF16),
        vm((2 * NX, width, 1024), BF16),
        vm((tok, width), F32),
        vm((2, OWN, 256, width), BF16),
        vm((RDR * blocks, BLOCK, width), BF16),
        vm((RDR * blocks, BLOCK, width), BF16),
        vm((RDR * blocks, 8, lanes), F32),
        vm((OWN, lanes, width), BF16),
        vm((OWN, lanes, width), BF16),
        vm((OWN, heads, 128, lanes), F32),
        vm((OWN, heads, 128, lanes), F32),
        vm((NY * OWN, 8, lanes), F32),
        vm((NY * OWN, 8, lanes), F32),
        vm((OWN, 8, lanes), F32),
        vm((OWN * RDR, BLOCK, width), BF16),
        vm((2, OWN, 256, width), BF16),
        vm((2, 4, 256, width), BF16),
        vm((2, 4, 256, width), BF16),
        vm((RDR * blocks, BLOCK, width), BF16),
        vm((8, BLOCK, width), BF16),
        vm((8, BLOCK, width), BF16),
        vm((8, BLOCK, width), BF16),
        pltpu.SMEM((2, 256), jnp.int32),
        pltpu.SMEM((8,), jnp.int32),
        pltpu.SMEM((288,), jnp.int32),
        pltpu.SemaphoreType.DMA((MAX_COPIES,)),
        pltpu.SemaphoreType.DMA((MAX_COPIES,)),
        pltpu.SemaphoreType.DMA((20,)),
    ]
    hbm = pl.BlockSpec(memory_space=pl.ANY)
    dq, dk_parts, dv = pl.pallas_call(
        functools.partial(body, heads),
        out_shape=(
            jax.ShapeDtypeStruct((blocks, BLOCK, width), BF16),
            jax.ShapeDtypeStruct((3, 256, width), BF16),
            jax.ShapeDtypeStruct((256, width), BF16),
        ),
        in_specs=[hbm] * 7,
        out_specs=(hbm, hbm, hbm),
        scratch_shapes=scratch,
        compiler_params=pltpu.CompilerParams(
            collective_id=0, has_side_effects=True, vmem_limit_bytes=63 * 1024 * 1024
        ),
        name="column_attention_grad",
    )(
        retrieval.T,
        counts,
        out_grad,
        out_weight,
        queries.reshape(blocks, BLOCK, width),
        keys.reshape(256, width),
        values.reshape(256, width),
    )
    dq, dk, dv = pl.pallas_call(
        finish,
        out_shape=(
            jax.ShapeDtypeStruct((blocks, BLOCK, width), BF16),
            jax.ShapeDtypeStruct((256, width), BF16),
            jax.ShapeDtypeStruct((256, width), BF16),
        ),
        in_specs=[hbm, hbm, hbm],
        out_specs=(hbm, hbm, hbm),
        scratch_shapes=[
            vm((blocks, BLOCK, width), BF16),
            vm((3, 256, width), BF16),
            vm((256, width), BF16),
            vm((256, width), BF16),
            pltpu.SemaphoreType.DMA((6,)),
        ],
        name="finish_outputs",
    )(dq, dk_parts, dv)
    return dq.reshape(queries.shape), dk.reshape(keys.shape), dv.reshape(values.shape)


def solution(mesh):
    return jax.shard_map(
        on_device,
        mesh=mesh,
        in_specs=(
            P("seq", "mp"),
            P("mp", None),
            P("seq", "mp"),
            P("seq", None, "mp"),
            P("seq", None, "mp"),
            P(),
            P("seq"),
        ),
        out_specs=(P("seq", "mp"), P("seq", None, "mp"), P("seq", None, "mp")),
        check_vma=False,
    )
```

```python
import functools
import math

import jax
import jax.numpy as jnp
from jax import lax
from jax.experimental import pallas as pl
from jax.experimental.pallas import tpu as pltpu
from jax.sharding import PartitionSpec as P

HEAD = 128
BLOCK = 64
NEIGH = 2
NX, NY, NZ = 4, 4, 8
OWN = NZ
RDR = NY
LOW = -1e30
MESH = pl.DeviceIdType.MESH
F32, BF16 = jnp.float32, jnp.bfloat16
NT = (((1,), (1,)), ((), ()))
NN = (((1,), (0,)), ((), ()))
TN = (((0,), (0,)), ((), ()))


class Ids:
    def __init__(self):
        self.at = {}

    def __call__(self, *name):
        return self.at.setdefault(name, len(self.at))


MAX_COPIES = 144
GROUPS = ((0, 0, 2), (1, 2, 2), (2, 4, 2), (3, 6, 1), (4, 7, 1))
HALVES = ((0, 0, 4), (1, 4, 4))
LOCAL_IN = 14
BLK, OTHER, PAIR, MINE, EXISTS, PLACE, PARITY = 0, 32, 64, 128, 192, 224, 256


def body(
    heads,
    ret_in,
    cnt_hbm,
    og_in,
    w_in,
    q_in,
    k_in,
    v_in,
    dq_out,
    dk_out,
    dv_out,
    og,
    w,
    acc,
    kv,
    q_all,
    do_all,
    cnt_all,
    q_own,
    do_own,
    ex,
    gw,
    low,
    st1,
    st2,
    fac,
    dqp,
    dkv,
    rsr,
    rsl,
    dqb,
    dq_far,
    dq_r,
    dq_l,
    ret,
    cnt_in,
    scal,
    ssem,
    rsem,
    lsem,
):
    ids = Ids()
    scale = 1.0 / math.sqrt(HEAD)
    seq, mp = lax.axis_index("seq"), lax.axis_index("mp")
    y, z = seq // NZ, seq % NZ
    x, core = mp // 2, mp % 2

    def at_x(d):
        return (seq, ((x + d) % NX) * 2 + core)

    sibling = (seq, x * 2 + (1 - core))

    def at_y(d):
        return (((y + d) % NY) * NZ + z, mp)

    def at_z(d):
        return (y * NZ + (z + d) % NZ, mp)

    def zz(d):
        return (z + d) % NZ

    started = []
    drained = [0]

    def drain(leave=0):
        for cp in started[drained[0] : len(started) - leave]:
            cp.wait_send()
        drained[0] = max(drained[0], len(started) - leave)

    def send(name, src, dst, dev):
        i = ids(*name)
        cp = pltpu.make_async_remote_copy(
            src_ref=src, dst_ref=dst, send_sem=ssem.at[i], recv_sem=rsem.at[i], device_id=dev, device_id_type=MESH
        )
        cp.start()
        started.append(cp)

    def recv(name, dst):
        i = ids(*name)
        pltpu.make_async_remote_copy(
            src_ref=dst, dst_ref=dst, send_sem=ssem.at[i], recv_sem=rsem.at[i], device_id=sibling, device_id_type=MESH
        ).wait_recv()

    barrier = pltpu.get_barrier_semaphore()
    peers = [at_x(1), at_x(-1), sibling, at_y(1), at_y(-1), at_y(2), at_z(1), at_z(-1)]
    for dev in peers:
        pl.semaphore_signal(barrier, inc=1, device_id=dev, device_id_type=MESH)

    local = []

    def local_copy(src, dst):
        cp = pltpu.make_async_copy(src, dst, lsem.at[len(local)])
        cp.start()
        local.append(cp)

    local_copy(ret_in, ret)
    local_copy(cnt_hbm, cnt_in)
    local_copy(og_in, og.at[mp])
    for c in range(2 * NX):
        local_copy(w_in.at[:, pl.ds(c * 1024, 1024)], w.at[c])
    local_copy(q_in, q_all.at[pl.ds(y * 8, 8)])
    local_copy(k_in, kv.at[0, z])
    local_copy(v_in, kv.at[1, z])

    def tables(r, carry):
        base = (r * NZ + z) * 8
        named = [ret[j % 2, base + j // 2] for j in range(16)]
        owner = [e >> 1 for e in named]
        code = []
        for j in range(16):
            own = owner[j] - y * OWN
            near = (own >= 0) & (own < OWN)
            scal[PAIR + r * 16 + j] = jnp.where(near, own, 0) * RDR + r
            scal[MINE + r * 16 + j] = jnp.where(near, 1, 0)
            code.append((owner[j ^ 1] << 5) + ((named[j] & 1) << 4) + ((j % 2) << 3) + j // 2 + 1024)
        for o in range(OWN):
            t = 0
            for j in range(16):
                t = t + jnp.where(owner[j] == y * OWN + o, code[j], 0)
            scal[BLK + o * RDR + r] = r * 8 + (t & 7)
            scal[PLACE + o * RDR + r] = (t >> 3) & 1
            scal[PARITY + o * RDR + r] = (t >> 4) & 1
            scal[OTHER + o * RDR + r] = (t >> 5) & 31
            scal[EXISTS + o * RDR + r] = t >> 10
        return carry

    def count_rows():
        for b in range(8):
            cnt_all[y * 8 + b] = jnp.full((8, RDR * BLOCK), cnt_in[b].astype(F32))


    pl.semaphore_wait(barrier, len(peers))

    def kv_piece(a, o, e):
        return kv.at[a, o, pl.ds(e * 128, 128)]

    pieces = [(a, e) for a in range(2) for e in range(2)]

    def kv_first():
        for a, e in pieces:
            src = (k_in, v_in)[a].at[pl.ds(e * 128, 128)]
            send(("kvR", 1, a, e), src, kv_piece(a, z, e), at_z(1))
            send(("kvL", 1, a, e), src, kv_piece(a, z, e), at_z(-1))

    def kv_hop(k, a):
        for e in range(2):
            if k < 4 or e == 0:
                o = zz(-k)
                recv(("kvR", k, a, e), kv_piece(a, o, e))
                if k < 3 or (k == 3 and e == 0):
                    send(("kvR", k + 1, a, e), kv_piece(a, o, e), kv_piece(a, o, e), at_z(1))
            if k < 4 or e == 1:
                o = zz(k)
                recv(("kvL", k, a, e), kv_piece(a, o, e))
                if k < 3 or (k == 3 and e == 1):
                    send(("kvL", k + 1, a, e), kv_piece(a, o, e), kv_piece(a, o, e), at_z(-1))

    def y_rows(d, part):
        return pl.ds(((y + d) % NY) * 8 + part[1], part[2])

    def y_first(tag, src, buf, part, way):
        send((tag, way, part[0]), src, buf.at[y_rows(0, part)], at_y(1 if way == "R" else -1))

    def y_on(tag, buf, part):
        even = part[0] % 2 == 0
        rows = buf.at[y_rows(-1 if even else 1, part)]
        recv((tag, "R" if even else "L", part[0]), rows)
        send((tag, "F", part[0]), rows, rows, at_y(1 if even else -1))

    def y_rest(tag, buf, part):
        even = part[0] % 2 == 0
        recv((tag, "L" if even else "R", part[0]), buf.at[y_rows(1 if even else -1, part)])
        recv((tag, "F", part[0]), buf.at[y_rows(2, part)])

    def y_direct(tag, src, buf, rows):
        mine = buf.at[pl.ds(y * rows, rows)]
        for d in (1, -1, 2):
            send((tag, d), src if src is not None else mine, mine, at_y(d))

    def y_direct_wait(tag, buf, rows):
        for d in (1, -1, 2):
            recv((tag, d), buf.at[pl.ds(((y - d) % NY) * rows, rows)])

    def og_piece(d, g, i=None, other=False):
        c = ((x + d) % NX) * 2 + ((1 - core) if other else core)
        return og.at[c, og_rows(g, i)]

    def og_rows(g, i=None):
        _, b0, n = GROUPS[g]
        if i is None:
            return pl.ds(b0 * BLOCK, n * BLOCK)
        return pl.ds(b0 * BLOCK + i * (n * BLOCK // 2), n * BLOCK // 2)

    def x_own(way, g, i):
        if g < len(GROUPS):
            send(("og", way, g, i), og_in.at[og_rows(g, i)], og_piece(0, g, i), at_x(1 if way == "R" else -1))

    def x_start():
        for n in range(3):
            x_own("R", n // 2, n % 2)
            x_own("L", n // 2, 1 - n % 2)

    def x_on(g):
        for way, i, d in (("R", 0, -1), ("L", 1, 1)):
            piece = og_piece(d, g, i)
            recv(("og", way, g, i), piece)
            send(("og", "F", g, i), piece, piece, at_x(-d))
            x_own(way, g + 1, 1 - i)
            x_own(way, g + 2, i)

    def x_near(g):
        for way, i, d in (("R", 1, -1), ("L", 0, 1)):
            recv(("og", way, g, i), og_piece(d, g, i))
            piece = og_piece(d, g)
            send(("ogc", d, g), piece, piece, sibling)

    def x_far(g):
        for i in range(2):
            recv(("og", "F", g, i), og_piece(2, g, i))
        piece = og_piece(2, g)
        send(("ogc", 2, g), piece, piece, sibling)

    def mm_own():
        for c in (mp, x * 2 + 1 - core):
            p = lax.dot_general(og[c], w[c], NT, preferred_element_type=F32)
            if c is mp:
                acc[...] = p
                recv(("ogc", 0), og.at[x * 2 + 1 - core])
            else:
                acc[...] += p

    def mm(d, g):
        rows = og_rows(g)
        for other in (False, True):
            c = ((x + d) % NX) * 2 + ((1 - core) if other else core)
            if other:
                recv(("ogc", d, g), og_piece(d, g, None, True))
            acc[rows, :] += lax.dot_general(og[c, rows, :], w[c], NT, preferred_element_type=F32)

    def grad_done(g):
        n = GROUPS[g][2]
        do_all[y_rows(0, GROUPS[g])] = acc[og_rows(g), :].astype(BF16).reshape(n, BLOCK, heads * HEAD)
        src = do_all.at[y_rows(0, GROUPS[g])]
        for way in ("R", "L"):
            y_first("do", src, do_all, GROUPS[g], way)

    def do_on(g):
        y_on("do", do_all, GROUPS[g])

    lane_reader = lax.broadcasted_iota(jnp.int32, (8, RDR * BLOCK), 1) // BLOCK

    def lane_pick(base, o):
        t = jnp.full((8, RDR * BLOCK), scal[base + o * RDR])
        for r in range(1, RDR):
            t = jnp.where(lane_reader == r, scal[base + o * RDR + r], t)
        return t.astype(F32)[0:1]

    def gather_blocks(src, dst, o):
        for r in range(RDR):
            dst[o, pl.ds(r * BLOCK, BLOCK), :] = src[scal[BLK + o * RDR + r]]

    def partner_rows(buf, o, base):
        t = buf[scal[base + o * RDR]]
        for r in range(1, RDR):
            t = jnp.where(lane_reader == r, buf[scal[base + o * RDR + r]], t)
        return t

    def cols(h):
        return pl.ds(h * HEAD, HEAD)

    def score_one(o):
        gather_blocks(q_all, q_own, o)
        par = lane_pick(PARITY, o)
        for h in range(heads):
            s = lax.dot_general(kv[0, o, :, cols(h)], q_own[o, :, cols(h)], NT, preferred_element_type=F32)
            s = jnp.where(par > 0.5, s[128:], s[:128]) * scale
            m = jnp.max(s, axis=0, keepdims=True)
            e = jnp.exp(s - m)
            ex[o, h] = e
            st1[y * OWN + o, h : h + 1, :] = m
            st1[y * OWN + o, heads + h : heads + h + 1, :] = jnp.sum(e, axis=0, keepdims=True)

    def scores(dist):
        if dist in (0, 4):
            score_one(zz(dist))
        else:

            def one(i, carry):
                score_one(zz(dist * (1 - 2 * i)))
                return carry

            lax.fori_loop(0, 2, one, 0)

    def lives(o):
        exists, place = lane_pick(EXISTS, o), lane_pick(PLACE, o)
        short = 2.0 - partner_rows(cnt_all, o, BLK)[0:1, :]
        return exists * (1.0 - place * short) > 0.5, exists * (1.0 - (1.0 - place) * short) > 0.5

    def factors():
        def one(o, carry):
            live, live_p = lives(o)
            own = st1[y * OWN + o]
            oth = partner_rows(st1, o, OTHER)
            m_o, l_o = own[:heads], own[heads : 2 * heads]
            m_p = jnp.where(live_p, oth[:heads], LOW)
            l_p = jnp.where(live_p, oth[heads : 2 * heads], 0.0)
            m = jnp.maximum(m_o, m_p)
            a = jnp.exp(m_o - m)
            f = jnp.where(live, a / (l_o * a + l_p * jnp.exp(m_p - m)), 0.0)
            par = lane_pick(PARITY, o)
            fac[o, 0:heads, :] = f * (1.0 - par)
            fac[o, heads : 2 * heads, :] = f * par
            return carry

        lax.fori_loop(0, OWN, one, 0)

    def both(o, h, t0, t1):
        return jnp.concatenate([t0.astype(BF16), t1.astype(BF16)], axis=0)

    def weights(o, h):
        e = ex[o, h]
        return both(o, h, e * fac[o, h : h + 1, :], e * fac[o, heads + h : heads + h + 1, :])

    def weights_one(o):
        for h in range(heads):
            low[o, h] = weights(o, h)

    def value_with(o, of):
        gather_blocks(do_all, do_own, o)
        for h in range(heads):
            t = lax.dot_general(of(o, h), do_own[o, :, cols(h)], NN, preferred_element_type=F32)
            dkv[1, o, :, cols(h)] = t.astype(BF16)

    def value_one(o):
        value_with(o, weights)

    def value_first(o):
        value_with(o, lambda o, h: low[o, h])

    def dots_one(o):
        par = lane_pick(PARITY, o)
        for h in range(heads):
            g = lax.dot_general(kv[1, o, :, cols(h)], do_own[o, :, cols(h)], NT, preferred_element_type=F32)
            g = jnp.where(par > 0.5, g[128:], g[:128])
            gw[o, h] = g
            f = fac[o, h : h + 1, :] + fac[o, heads + h : heads + h + 1, :]
            p = (ex[o, h] * f).astype(BF16).astype(F32)
            st2[y * OWN + o, h : h + 1, :] = jnp.sum(p * g, axis=0, keepdims=True)

    def key_one(o):
        _, live_p = lives(o)
        rd = st2[y * OWN + o][:heads] + jnp.where(live_p, partner_rows(st2, o, OTHER)[:heads], 0.0)
        for h in range(heads):
            e = ex[o, h]
            t = gw[o, h] - rd[h : h + 1]
            d = both(o, h, e * fac[o, h : h + 1, :] * t, e * fac[o, heads + h : heads + h + 1, :] * t)
            dk = lax.dot_general(d, q_own[o, :, cols(h)], NN, preferred_element_type=F32)
            dkv[0, o, :, cols(h)] = (dk * scale).astype(BF16)
            dq = lax.dot_general(d, kv[0, o, :, cols(h)], TN, preferred_element_type=F32)
            dqp[pl.ds(o * RDR, RDR), :, cols(h)] = (dq * scale).astype(BF16).reshape(RDR, BLOCK, HEAD)

    def per_owner(fn, dist):
        if dist in (0, 4):
            fn(zz(dist))
        else:

            def one(i, carry):
                fn(zz(dist * (1 - 2 * i)))
                return carry

            lax.fori_loop(0, 2, one, 0)

    def rs_buf(way, a, k, e):
        rows = pl.ds(e * 128, 128)
        if k == 3 and a == 0:
            return dk_out.at[1 if way == "R" else 2, rows]
        return (rsr if way == "R" else rsl).at[a, k, rows]

    def rs_hop(way, a, k, e):
        far = 0 if way == "R" else 1
        sign = 1 if way == "R" else -1
        o = zz(sign * (4 - k))
        piece = dkv.at[a, o, pl.ds(e * 128, 128)]
        if k > 1 or (k == 1 and e == far):
            rs_take(way, a, k - 1, e, o)
        send(("rs" + way, a, k, e), piece, rs_buf(way, a, k, e), at_z(sign))

    def rs_take(way, a, k, e, o):
        buf = rsr if way == "R" else rsl
        recv(("rs" + way, a, k, e), rs_buf(way, a, k, e))
        rows = pl.ds(e * 128, 128)
        dkv[a, o, rows, :] = (dkv[a, o, rows, :].astype(F32) + buf[a, k, rows, :].astype(F32)).astype(BF16)

    def rs_far(a, k):
        rs_hop("R", a, k, 0)
        rs_hop("L", a, k, 1)

    def rs_near(a, k):
        rs_hop("R", a, k, 1)
        rs_hop("L", a, k, 0)

    x_start()
    kv_first()
    for h in range(2):
        for way, part in (("R", HALVES[h]), ("L", HALVES[1 - h])):
            y_first("q", q_in.at[pl.ds(part[1], part[2])], q_all, part, way)
    send(("ogc", 0), og_in, og.at[mp], sibling)
    for cp in local[:2]:
        cp.wait()
    count_rows()
    y_direct("cnt", None, cnt_all, 8)
    lax.fori_loop(0, RDR, tables, 0)

    x_on(0)
    for part in HALVES:
        y_on("q", q_all, part)
    kv_hop(1, 0)
    x_near(0)
    for cp in local[2:]:
        cp.wait()
    x_on(1)
    mm_own()
    kv_hop(1, 1)
    x_far(0)
    for d in (-1, 1, 2):
        mm(d, 0)
    grad_done(0)
    x_near(1)
    for part in HALVES:
        y_rest("q", q_all, part)
    y_direct_wait("cnt", cnt_all, 8)
    x_on(2)
    kv_hop(2, 0)
    scores(0)
    for d in (-1, 1):
        mm(d, 1)
    x_far(1)
    mm(2, 1)
    grad_done(1)
    do_on(0)
    x_near(2)
    kv_hop(2, 1)
    x_on(3)
    for d in (-1, 1):
        mm(d, 2)
    scores(1)
    x_far(2)
    mm(2, 2)
    grad_done(2)
    do_on(1)
    kv_hop(3, 0)
    x_near(3)
    x_on(4)
    for d in (-1, 1):
        mm(d, 3)
    x_far(3)
    mm(2, 3)
    grad_done(3)
    x_near(4)
    do_on(2)
    for d in (-1, 1):
        mm(d, 4)
    x_far(4)
    kv_hop(3, 1)
    mm(2, 4)
    grad_done(4)
    scores(2)
    do_on(3)
    scores(3)
    kv_hop(4, 0)
    scores(4)
    y_direct("st1", None, st1, OWN)
    do_on(4)
    kv_hop(4, 1)
    for g in range(4):
        y_rest("do", do_all, GROUPS[g])
    y_direct_wait("st1", st1, OWN)
    factors()
    for d in (4, 3):
        per_owner(weights_one, d)
    y_rest("do", do_all, GROUPS[4])

    per_owner(value_first, 4)
    rs_far(1, 0)
    per_owner(value_first, 3)
    rs_near(1, 1)
    for d in (2, 1, 0):
        per_owner(value_one, d)
    for d in (4, 3, 2, 1, 0):
        per_owner(dots_one, d)
    y_direct("st2", None, st2, OWN)
    rs_far(1, 1)
    rs_near(1, 2)
    rs_far(1, 2)
    drain(14)
    y_direct_wait("st2", st2, OWN)

    per_owner(key_one, 4)
    rs_far(0, 0)
    per_owner(key_one, 3)
    rs_near(0, 1)
    rs_near(1, 3)
    per_owner(key_one, 2)
    rs_far(0, 1)
    per_owner(key_one, 1)
    rs_near(0, 2)
    rs_far(1, 3)
    per_owner(key_one, 0)
    local_copy(dkv.at[0, z], dk_out.at[0])

    def blocks(r, carry):
        def one(b, carry2):
            j = r * 16 + b * 2
            t = dqp[scal[PAIR + j]].astype(F32) * scal[MINE + j].astype(F32)
            t += dqp[scal[PAIR + 1 + j]].astype(F32) * scal[MINE + 1 + j].astype(F32)
            dqb[r * 8 + b] = t.astype(BF16)
            return carry2

        return lax.fori_loop(0, 8, one, carry)

    lax.fori_loop(0, RDR, blocks, 0)

    def dq_rows(d, h):
        return dqb.at[y_rows(d, HALVES[h])]

    def dq_land(way, h):
        return (dq_r if way == "R" else dq_l).at[pl.ds(h * 4, 4)]

    send(("dq", "R", "far"), dq_rows(2, 0), dq_far.at[pl.ds(0, 4)], at_y(1))
    send(("dq", "L", "far"), dq_rows(2, 1), dq_far.at[pl.ds(4, 4)], at_y(-1))
    send(("dq", "R", 1), dq_rows(1, 1), dq_land("R", 1), at_y(1))
    send(("dq", "L", 0), dq_rows(-1, 0), dq_land("L", 0), at_y(-1))

    def dq_on(way, h, d):
        far = pl.ds(h * 4, 4)
        recv(("dq", way, "far"), dq_far.at[far])
        rows = y_rows(d, HALVES[h])
        dqb[rows] = (dqb[rows].astype(F32) + dq_far[far].astype(F32)).astype(BF16)
        send(("dq", way, h), dqb.at[rows], dq_land(way, h), at_y(d))

    rs_far(0, 2)
    rs_near(0, 3)
    dq_on("R", 0, 1)
    dq_on("L", 1, -1)
    rs_far(0, 3)

    def rs_last(a):
        for e in range(2):
            for way in ("R", "L"):
                recv(("rs" + way, a, 3, e), rs_buf(way, a, 3, e))

    def three(a, b, c):
        return (a.astype(F32) + b.astype(F32) + c.astype(F32)).astype(BF16)

    rs_last(1)
    dkv[1, z] = three(dkv[1, z], rsr[1, 3], rsl[1, 3])
    local_copy(dkv.at[1, z], dv_out)
    for h in range(2):
        for way in ("R", "L"):
            recv(("dq", way, h), dq_land(way, h))
    own = pl.ds(y * 8, 8)
    dqb[own] = three(dqb[own], dq_r[...], dq_l[...])
    local_copy(dqb.at[own], dq_out)
    drain(4)
    for cp in local[LOCAL_IN:]:
        cp.wait()
    rs_last(0)
    drain()


def finish(dq_in, dk_in, dv_in, dq_out, dk_out, dv_out, dq, dk, dv, total, sem):
    takes = [
        pltpu.make_async_copy(src, dst, sem.at[i])
        for i, (src, dst) in enumerate(((dk_in, dk), (dv_in, dv), (dq_in, dq)))
    ]
    gives = [
        pltpu.make_async_copy(src, dst, sem.at[3 + i])
        for i, (src, dst) in enumerate(((total, dk_out), (dv, dv_out), (dq, dq_out)))
    ]
    for take in takes:
        take.start()
    takes[0].wait()
    total[...] = (dk[0].astype(F32) + dk[1].astype(F32) + dk[2].astype(F32)).astype(BF16)
    gives[0].start()
    for i in (1, 2):
        takes[i].wait()
        gives[i].start()
    for give in gives:
        give.wait()


def on_device(out_grad, out_weight, queries, keys, values, retrieval, counts):
    tok, width = queries.shape
    heads = width // HEAD
    blocks = tok // BLOCK
    lanes = NY * BLOCK
    vm = pltpu.VMEM
    scratch = [
        vm((2 * NX, tok, 1024), BF16),
        vm((2 * NX, width, 1024), BF16),
        vm((tok, width), F32),
        vm((2, OWN, 256, width), BF16),
        vm((RDR * blocks, BLOCK, width), BF16),
        vm((RDR * blocks, BLOCK, width), BF16),
        vm((RDR * blocks, 8, lanes), F32),
        vm((OWN, lanes, width), BF16),
        vm((OWN, lanes, width), BF16),
        vm((OWN, heads, 128, lanes), F32),
        vm((OWN, heads, 128, lanes), F32),
        vm((OWN, heads, 256, lanes), BF16),
        vm((NY * OWN, 8, lanes), F32),
        vm((NY * OWN, 8, lanes), F32),
        vm((OWN, 8, lanes), F32),
        vm((OWN * RDR, BLOCK, width), BF16),
        vm((2, OWN, 256, width), BF16),
        vm((2, 4, 256, width), BF16),
        vm((2, 4, 256, width), BF16),
        vm((RDR * blocks, BLOCK, width), BF16),
        vm((8, BLOCK, width), BF16),
        vm((8, BLOCK, width), BF16),
        vm((8, BLOCK, width), BF16),
        pltpu.SMEM((2, 256), jnp.int32),
        pltpu.SMEM((8,), jnp.int32),
        pltpu.SMEM((288,), jnp.int32),
        pltpu.SemaphoreType.DMA((MAX_COPIES,)),
        pltpu.SemaphoreType.DMA((MAX_COPIES,)),
        pltpu.SemaphoreType.DMA((20,)),
    ]
    hbm = pl.BlockSpec(memory_space=pl.ANY)
    dq, dk_parts, dv = pl.pallas_call(
        functools.partial(body, heads),
        out_shape=(
            jax.ShapeDtypeStruct((blocks, BLOCK, width), BF16),
            jax.ShapeDtypeStruct((3, 256, width), BF16),
            jax.ShapeDtypeStruct((256, width), BF16),
        ),
        in_specs=[hbm] * 7,
        out_specs=(hbm, hbm, hbm),
        scratch_shapes=scratch,
        compiler_params=pltpu.CompilerParams(
            collective_id=0, has_side_effects=True, vmem_limit_bytes=63 * 1024 * 1024
        ),
        name="column_attention_grad",
    )(
        retrieval.T,
        counts,
        out_grad,
        out_weight,
        queries.reshape(blocks, BLOCK, width),
        keys.reshape(256, width),
        values.reshape(256, width),
    )
    dq, dk, dv = pl.pallas_call(
        finish,
        out_shape=(
            jax.ShapeDtypeStruct((blocks, BLOCK, width), BF16),
            jax.ShapeDtypeStruct((256, width), BF16),
            jax.ShapeDtypeStruct((256, width), BF16),
        ),
        in_specs=[hbm, hbm, hbm],
        out_specs=(hbm, hbm, hbm),
        scratch_shapes=[
            vm((blocks, BLOCK, width), BF16),
            vm((3, 256, width), BF16),
            vm((256, width), BF16),
            vm((256, width), BF16),
            pltpu.SemaphoreType.DMA((6,)),
        ],
        name="finish_outputs",
    )(dq, dk_parts, dv)
    return dq.reshape(queries.shape), dk.reshape(keys.shape), dv.reshape(values.shape)


def solution(mesh):
    return jax.shard_map(
        on_device,
        mesh=mesh,
        in_specs=(
            P("seq", "mp"),
            P("mp", None),
            P("seq", "mp"),
            P("seq", None, "mp"),
            P("seq", None, "mp"),
            P(),
            P("seq"),
        ),
        out_specs=(P("seq", "mp"), P("seq", None, "mp"), P("seq", None, "mp")),
        check_vma=False,
    )
```
